256 devices in a mesh: dp: 4 (over x), expert: 64 (over y, z, core).
Axes of the slice: x: 4, y: 4, z: 8, core: 2. Of those that a mesh axis runs over, the one named last changes fastest.
Arguments:
- tokens: bfloat16 [4096, 3584], P(('dp', 'expert')), may hold values from -6 to 6
- out_grad: bfloat16 [4096, 3584], P(('dp', 'expert')), may hold values from -6 to 6
- route_ids: int32 [4096, 8], P(('dp', 'expert')), may hold values from 0 to 127, all different within a row; in each aligned block of 16 rows (0 to 15, 16 to 31, ...) at most 2 rows name the same one
- route_probs: float32 [4096, 8], P(('dp', 'expert')), may hold values from 0.02 to 0.5
- w_gate: bfloat16 [128, 3584, 1024], P('expert', None, 'dp'), may hold values from -0.09375 to 0.09375
- w_up: bfloat16 [128, 3584, 1024], P('expert', None, 'dp'), may hold values from -0.09375 to 0.09375
- w_down: bfloat16 [128, 1024, 3584], P('expert', 'dp'), may hold values from -0.1875 to 0.1875
Outputs:
- in_grad: bfloat16 [4096, 3584], P(('dp', 'expert'))
The draws below stay inside these ranges and needn't reach their ends.
Inputs may be any that keep to these rules, and one draw needn't show every extreme that they name: `route_ids`: the 8 ids of a token differ. Among the tokens of one device (aligned blocks of 16 rows) no expert is named more than 2 times, and in every draw some expert is named exactly 2 times there.
All inputs are finite; a program needn't handle non-finite values.
Results may differ from the reference program's by a relative error of at most 0.015.
Values may be sent and summed in bfloat16 or wider, within the bound.
No kernel may reach another device: no remote copies, remote signals or barrier semaphores. Data moves between devices by JAX's collectives and lax.ppermute only.
A program may use at most 128 MiB of HBM per device.

```python
import math
import jax
import jax.numpy as jnp
import numpy as np
from jax import lax

D = 3584
H = 1024
TOPK = 8
TOK_DEV = 16
EXPERTS = 128
CAP = 2
TOKENS = 4096
N_DP = 4


def block_scale(stream_key, dims, cuts, smallest, top_value):
    loudness, own = 1.0, jax.random.fold_in(stream_key, 6)
    for axis_at, blocks in cuts:
        heights = jnp.exp(jax.random.uniform(jax.random.fold_in(own, axis_at), (blocks,), jnp.float32, smallest / len(cuts), top_value / len(cuts)))
        loudness = loudness * jnp.repeat(heights, dims[axis_at] // blocks).reshape([-1 if axis == axis_at else 1 for axis in range(len(dims))])
    return loudness


def shared_out(key, own, number, rows, amount, top, bound, slope):
    order = jax.random.permutation(key, amount)
    packed, ordinary = portions_of(amount, rows * top, bound, slope, True), portions_of(amount, rows * top, bound, slope, False)
    places = jnp.arange(amount)

    def named(sizes, rotation):
        used = int((sizes > 0).sum())
        fixed = max(1, used // 4)
        shifted = fixed + (places - fixed + rotation * (used - fixed)) % max(1, amount - fixed)
        return jnp.zeros((amount,), jnp.int32).at[order[jnp.where(places < fixed, places, shifted)]].set(jnp.asarray(sizes, jnp.int32))

    sizes = jnp.where(number % 4 == 0, named(packed, number // 4), named(ordinary, number - number // 4 - 1))
    mixed = jax.random.permutation(jax.random.fold_in(own, 3), amount)
    giver, sink = mixed[0:amount // 2 * 2:2], mixed[1:amount // 2 * 2:2]
    room = jnp.minimum(sizes[giver] - 1, bound - sizes[sink]) // 2
    room = jnp.where((giver == order[0]) | (sink == order[0]) | (sizes[sink] == 0), 0, jnp.maximum(room, 0))
    shifted = jax.random.randint(jax.random.fold_in(own, 4), (amount // 2,), 0, 1 << 20) % (room + 1)
    sizes = sizes.at[giver].add(-shifted).at[sink].add(shifted)
    members = jnp.searchsorted(jnp.cumsum(sizes), jnp.arange(rows * top), side="right").astype(jnp.int32)
    grid = members.reshape(top, rows).T
    grid = grid[jax.random.permutation(jax.random.fold_in(own, 1), rows)]
    rotation = jax.random.randint(jax.random.fold_in(own, 2), (rows, 1), 0, top)
    return jnp.take_along_axis(grid, (jnp.arange(top)[None, :] + rotation) % top, axis=1)


def portions_of(number_of, total, limit, slope, full):
    weights = [(1 << 20) // math.isqrt(rank ** slope) + 1 for rank in range(1, number_of + 1)]
    largest = limit if full else min(limit, max(-(-total // number_of), total * weights[0] // sum(weights)))
    least = 1 if total - largest >= number_of - 1 else 0
    holding, surplus = [largest] + [least] * (number_of - 1), total - largest - least * (number_of - 1)
    while surplus > 0:
        movable = [i for i in range(1, number_of) if holding[i] < largest] or [i for i in range(1, number_of) if holding[i] < limit]
        mass, left = sum([weights[i] for i in movable]), surplus
        for i in movable:
            more = min(limit - holding[i], max(1, left * weights[i] // mass), surplus)
            holding[i] = holding[i] + more
            surplus = surplus - more
    return np.array(holding)


def gaussian(key, dims, scale, most, cuts=(), held_as=jnp.bfloat16):
    values = scale * jax.random.normal(key, dims, jnp.float32)
    if cuts:
        values = values * block_scale(key, dims, cuts, -0.22, 0.18)
    return jnp.clip(values, -most, most).astype(held_as)


def setup_inputs(seed: int = 0) -> dict:
    keys = jax.random.split(jax.random.key(seed), 8)
    tokens = gaussian(keys[0], (TOKENS, D), 1.0, 6.0, ((0, 256),))
    out_grad = gaussian(keys[1], (TOKENS, D), 1.0, 6.0, ((0, 256),))
    route_ids_keys = jax.random.split(jax.random.fold_in(keys[2], 1), TOKENS // TOK_DEV)
    route_ids_turns = jax.random.permutation(jax.random.fold_in(keys[2], 3), TOKENS // TOK_DEV)
    route_ids = jax.vmap(lambda own, number: shared_out(jax.random.fold_in(keys[2], 2), own, number, TOK_DEV, EXPERTS, TOPK, CAP, 2))(route_ids_keys, route_ids_turns).reshape((TOKENS, TOPK))
    route_probs = jnp.clip(jnp.exp(math.log(0.5) - 3.218876 * jax.random.uniform(keys[3], (TOKENS, TOPK), jnp.float32) ** block_scale(keys[3], (TOKENS, TOPK), ((0, 256),), -0.2, 0.2)), 0.02, 0.5)
    w_gate = gaussian(keys[4], (EXPERTS, D, H), D ** -0.5, 0.09375, ((0, 64), (2, 4)))
    w_up = gaussian(keys[5], (EXPERTS, D, H), D ** -0.5, 0.09375, ((0, 64), (2, 4)))
    w_down = gaussian(keys[6], (EXPERTS, H, D), H ** -0.5, 0.1875, ((0, 64), (1, 4)))
    return dict(tokens=tokens, out_grad=out_grad, route_ids=route_ids, route_probs=route_probs, w_gate=w_gate, w_up=w_up, w_down=w_down)


def reference(tokens, out_grad, route_ids, route_probs, w_gate, w_up, w_down):
    experts = w_gate.shape[0]
    tok_total = tokens.shape[0]
    width = tokens.shape[1]
    blocks = tok_total // TOK_DEV
    per_block = TOK_DEV * TOPK
    block_ids = route_ids.reshape(blocks, per_block)
    onehot = (block_ids[:, :, None] == jnp.arange(experts, dtype=jnp.int32)[None, None, :]).astype(jnp.int32)
    slot_rank = jnp.sum((jnp.cumsum(onehot, axis=1) - onehot) * onehot, axis=2)
    block_index = (jnp.arange(blocks * per_block, dtype=jnp.int32) // per_block).reshape(blocks, per_block)
    table_row = (block_index * CAP + slot_rank).reshape(-1)
    flat_expert = route_ids.reshape(-1)
    token_index = jnp.arange(tok_total * TOPK, dtype=jnp.int32) // TOPK
    table_width = blocks * CAP
    table = jnp.full((experts, table_width), tok_total, dtype=jnp.int32).at[flat_expert, table_row].set(token_index)
    weights = jnp.zeros((experts, table_width), jnp.float32).at[flat_expert, table_row].set(route_probs.reshape(-1))
    zero_row = jnp.zeros((1, width), tokens.dtype)
    padded_tokens = jnp.concatenate([tokens, zero_row], axis=0)
    padded_grads = jnp.concatenate([out_grad, zero_row], axis=0)
    quarter = w_gate.shape[2] // N_DP

    def one_expert(carry, expert):
        rows = table[expert]
        x_rows = padded_tokens[rows]
        g_rows = (padded_grads[rows].astype(jnp.float32) * weights[expert][:, None]).astype(jnp.bfloat16)
        gate_w = w_gate[expert]
        up_w = w_up[expert]
        down_w = w_down[expert]
        gate_pre = jnp.dot(x_rows, gate_w, preferred_element_type=jnp.float32)
        up_pre = jnp.dot(x_rows, up_w, preferred_element_type=jnp.float32)
        hidden_grad = jnp.dot(g_rows, down_w.T, preferred_element_type=jnp.float32)
        sigmoid_a = jax.nn.sigmoid(gate_pre)
        gate_grad = (hidden_grad * up_pre * sigmoid_a * (1.0 + gate_pre * (1.0 - sigmoid_a))).astype(jnp.bfloat16)
        up_grad = (hidden_grad * gate_pre * sigmoid_a).astype(jnp.bfloat16)
        total = jnp.zeros((rows.shape[0], width), jnp.float32)
        for block in range(N_DP):
            low = block * quarter
            high = low + quarter
            partial_value = jnp.dot(gate_grad[:, low:high], gate_w[:, low:high].T, preferred_element_type=jnp.float32)
            partial_value = partial_value + jnp.dot(up_grad[:, low:high], up_w[:, low:high].T, preferred_element_type=jnp.float32)
            total = total + partial_value.astype(jnp.bfloat16).astype(jnp.float32)
        return carry.at[rows].add(total), None

    start = jnp.zeros((tok_total + 1, width), jnp.float32)
    final, unused = lax.scan(one_expert, start, jnp.arange(experts, dtype=jnp.int32))
    return final[:tok_total].astype(jnp.bfloat16)
```

```python
import jax
import jax.numpy as jnp
from jax import lax
from jax.experimental import pallas as pl
from jax.experimental.pallas import tpu as pltpu
from jax.sharding import PartitionSpec as P

CAP = 2
LANES = 128
BLOCK = 256
CHUNKS = 2
NT = (((1,), (1,)), ((), ()))


def slot_table(ids, probs, experts):
    tok_count = ids.shape[0]
    named = ids.T[None, :, :] == jnp.arange(experts, dtype=jnp.int32)[:, None, None]
    mask = jnp.any(named, axis=1)
    scale = jnp.sum(jnp.where(named, probs.T[None, :, :], 0.0), axis=1)
    order = jnp.arange(tok_count, dtype=jnp.int32)
    before = (order[:, None] < order[None, :])[None, :, :]
    rank = jnp.sum((mask[:, :, None] & before).astype(jnp.int32), axis=1)
    slots = mask[:, None, :] & (rank[:, None, :] == jnp.arange(CAP, dtype=jnp.int32)[None, :, None])
    slot_scale = jnp.sum(jnp.where(slots, scale[:, None, :], 0.0), axis=2)
    return slots.reshape(experts * CAP, tok_count), slot_scale.reshape(experts * CAP)


def hidden_kernel(own_ref, right_ref, far_a_ref, far_b_ref, left_ref, w_ref, out_ref):
    width = w_ref.shape[2]
    half = own_ref.shape[0] // 2
    for e in range(2):
        rows = pl.ds(e * half, half)
        far = (far_a_ref, far_b_ref)[e]
        g = jnp.concatenate(
            [own_ref[rows, :width], right_ref[rows, :width], far[:, :width], left_ref[rows, :width]], axis=0
        )
        out_ref[e] = lax.dot_general(g, w_ref[e], NT, preferred_element_type=jnp.float32)


def hidden_grads(own, right, far_a, far_b, left, w_down):
    local_experts, units, width = w_down.shape
    rows = own.shape[0] // 2 * 4
    return pl.pallas_call(
        hidden_kernel,
        out_shape=jax.ShapeDtypeStruct((local_experts, rows, units), jnp.float32),
        in_specs=[pl.BlockSpec(memory_space=pltpu.VMEM)] * 6,
        out_specs=pl.BlockSpec(memory_space=pltpu.VMEM),
        cost_estimate=pl.CostEstimate(
            flops=2 * local_experts * rows * units * width, bytes_accessed=12 << 20, transcendentals=0
        ),
        name="hidden_grads",
    )(own, right, far_a, far_b, left, w_down)


def act_kernel(me_ref, x_ref, sel_ref, gate_ref, up_ref, hidden_ref, out_ref, picked):
    step = pl.program_id(0)
    blocks = pl.num_programs(0) // 4
    group, block = step // blocks, step % blocks
    rows = lax.dot_general(
        sel_ref[0], x_ref[...], (((1,), (0,)), ((), ())), preferred_element_type=jnp.float32
    ).astype(jnp.bfloat16)
    part = rows.shape[0] // 4
    for slot in range(4):
        at = pl.multiple_of(group * (blocks * part * CAP) + (slot % CAP) * (blocks * part) + block * part, 16)
        picked[slot // CAP, pl.ds(at, part), :] = rows[slot * part : (slot + 1) * part]

    @pl.when(step == pl.num_programs(0) - 1)
    def _():
        units = gate_ref.shape[2]
        for e in range(2):
            x = picked[e]
            gate_pre = jnp.dot(x, gate_ref[e], preferred_element_type=jnp.float32)
            up_pre = jnp.dot(x, up_ref[e], preferred_element_type=jnp.float32)
            hidden = hidden_ref[e]
            s = jax.nn.sigmoid(gate_pre)
            out_ref[e, :, :units] = (hidden * up_pre * s * (1.0 + gate_pre * (1.0 - s))).astype(jnp.bfloat16)
            out_ref[e, :, units:] = (hidden * gate_pre * s).astype(jnp.bfloat16)


def act_grads(me, x_all, sel, w_gate, w_up, hidden):
    local_experts, width, units = w_gate.shape
    steps, part, block = sel.shape
    rows = hidden.shape[1]
    blocks = steps // 4
    whole = lambda i, me: (0, 0, 0)
    return pl.pallas_call(
        act_kernel,
        out_shape=jax.ShapeDtypeStruct((local_experts, rows, 2 * units), jnp.bfloat16),
        grid_spec=pltpu.PrefetchScalarGridSpec(
            num_scalar_prefetch=1,
            grid=(steps,),
            in_specs=[
                pl.BlockSpec((block, width), lambda i, me: (lax.rem(me[0] + i // blocks, 4) * blocks + i % blocks, 0)),
                pl.BlockSpec((1, part, block), lambda i, me: (i, 0, 0)),
                pl.BlockSpec((local_experts, width, units), whole),
                pl.BlockSpec((local_experts, width, units), whole),
                pl.BlockSpec((local_experts, rows, units), whole),
            ],
            out_specs=pl.BlockSpec((local_experts, rows, 2 * units), whole),
            scratch_shapes=[pltpu.VMEM((local_experts, rows, width), jnp.bfloat16)],
        ),
        compiler_params=pltpu.CompilerParams(dimension_semantics=("arbitrary",)),
        cost_estimate=pl.CostEstimate(
            flops=2 * local_experts * rows * 2 * units * width + 2 * steps * part * block * width,
            bytes_accessed=40 << 20,
            transcendentals=local_experts * rows * units,
        ),
        name="act_grads",
    )(me, x_all, sel, w_gate, w_up, hidden)


def out_kernel(me_ref, h_ref, gate_ref, up_ref, out_ref):
    units = gate_ref.shape[2]
    for e in range(2):
        value = lax.dot_general(h_ref[e, :, :units], gate_ref[e], NT, preferred_element_type=jnp.float32)
        value = value + lax.dot_general(h_ref[e, :, units:], up_ref[e], NT, preferred_element_type=jnp.float32)
        value = value.astype(jnp.bfloat16)
        part = value.shape[0] // 4
        for r in range(4):
            out_ref[lax.rem(me_ref[0] + r, 4), e * part : (e + 1) * part, :] = value[r * part : (r + 1) * part]


def out_rows(me, h, w_gate, w_up, chunk, chunks, cols):
    local_experts, rows, _ = h.shape
    _, width, units = w_gate.shape
    per = width // chunks // cols
    first = chunk * per
    w_spec = pl.BlockSpec((local_experts, cols, units), lambda n, me: (0, first + n, 0))
    return pl.pallas_call(
        out_kernel,
        out_shape=jax.ShapeDtypeStruct((4, local_experts * rows // 4, width // chunks), jnp.bfloat16),
        grid_spec=pltpu.PrefetchScalarGridSpec(
            num_scalar_prefetch=1,
            grid=(per,),
            in_specs=[
                pl.BlockSpec((local_experts, rows, 2 * units), lambda n, me: (0, 0, 0)),
                w_spec,
                w_spec,
            ],
            out_specs=pl.BlockSpec((4, local_experts * rows // 4, cols), lambda n, me: (0, 0, n)),
        ),
        compiler_params=pltpu.CompilerParams(dimension_semantics=("arbitrary",)),
        cost_estimate=pl.CostEstimate(
            flops=2 * local_experts * rows * 2 * units * width // chunks, bytes_accessed=8 << 20, transcendentals=0
        ),
        name="out_rows",
    )(me, h, w_gate, w_up)


def on_device(tokens, out_grad, route_ids, route_probs, w_gate, w_up, w_down):
    columns = lax.axis_size("expert")
    local_experts = w_gate.shape[0]
    experts = local_experts * columns
    tok_count, width = tokens.shape
    slots = experts * CAP
    per_dest = local_experts * CAP
    me = lax.axis_index("dp").astype(jnp.int32).reshape(1)

    with jax.named_scope("gather_tokens"):
        x_all = lax.all_gather(tokens, ("dp", "expert"), axis=0, tiled=True)

    with jax.named_scope("build_slots"):
        table, slot_scale = slot_table(route_ids, route_probs, experts)
        select = table.astype(jnp.bfloat16)
        picked = jnp.dot(select, out_grad, preferred_element_type=jnp.float32)
        g_rows = (picked * slot_scale[:, None]).astype(jnp.bfloat16)
        which = jnp.sum(jnp.where(table, jnp.arange(1, tok_count + 1, dtype=jnp.int32)[None, :], 0), axis=1) - 1
        tag = jnp.broadcast_to(which.astype(jnp.bfloat16)[:, None], (slots, LANES))
        tiles = jnp.concatenate([g_rows, tag], axis=1).reshape(columns, per_dest, width + LANES)

    with jax.named_scope("send_slots"):
        got = lax.all_to_all(tiles, "expert", split_axis=0, concat_axis=0, tiled=True)
        own = got.transpose(1, 0, 2).reshape(slots, width + LANES)

    with jax.named_scope("ring"):
        up_ring = [(i, (i + 1) % 4) for i in range(4)]
        down_ring = [(i, (i + 3) % 4) for i in range(4)]
        half = slots // 2
        a, b = own[:half], own[half:]
        left_a = lax.ppermute(a, "dp", up_ring)
        right_b = lax.ppermute(b, "dp", down_ring)
        left_b = lax.ppermute(b, "dp", up_ring)
        right_a = lax.ppermute(a, "dp", down_ring)
        far_a = lax.ppermute(left_a, "dp", up_ring)
        far_b = lax.ppermute(right_b, "dp", down_ring)
        left = jnp.concatenate([left_a, left_b], axis=0)
        right = jnp.concatenate([right_a, right_b], axis=0)

    with jax.named_scope("token_choice"):
        tags = jnp.stack(
            [
                own[:, width],
                right[:, width],
                jnp.concatenate([far_a[:, width], far_b[:, width]]),
                left[:, width],
            ]
        )
        sources = BLOCK // tok_count
        blocks = columns // sources
        tags = tags.reshape(4, per_dest, blocks, sources).transpose(0, 2, 1, 3)
        target = tags.astype(jnp.int32) + jnp.where(
            tags < 0, -BLOCK, tok_count * jnp.arange(sources, dtype=jnp.int32)
        )
        target = target.reshape(4 * blocks, per_dest * sources)
        sel = (target[:, :, None] == jnp.arange(BLOCK, dtype=jnp.int32)).astype(jnp.bfloat16)

    hidden = hidden_grads(own, right, far_a, far_b, left, w_down)
    h = act_grads(me, x_all, sel, w_gate, w_up, hidden)

    results = []
    for chunk in range(CHUNKS):
        cols = width // CHUNKS
        partials = out_rows(me, h, w_gate, w_up, chunk, CHUNKS, 256)
        with jax.named_scope("sum_blocks"):
            summed = lax.psum_scatter(
                partials.reshape(4 * slots, cols), "dp", scatter_dimension=0, tiled=True
            )
        with jax.named_scope("return_slots"):
            back = summed.reshape(per_dest, columns, cols).transpose(1, 0, 2)
            returned = lax.all_to_all(back, "expert", split_axis=0, concat_axis=0, tiled=True)
        with jax.named_scope("combine"):
            results.append(
                lax.dot_general(
                    select, returned.reshape(slots, cols), (((0,), (0,)), ((), ())),
                    preferred_element_type=jnp.float32,
                ).astype(jnp.bfloat16)
            )
    return jnp.concatenate(results, axis=1)


def solution(mesh):
    placed = (
        P(("dp", "expert"), None),
        P(("dp", "expert"), None),
        P(("dp", "expert"), None),
        P(("dp", "expert"), None),
        P("expert", None, "dp"),
        P("expert", None, "dp"),
        P("expert", "dp", None),
    )
    return jax.shard_map(
        on_device, mesh=mesh, in_specs=placed, out_specs=P(("dp", "expert"), None), check_vma=False
    )
```

```python
import jax
import jax.numpy as jnp
from jax import lax
from jax.experimental import pallas as pl
from jax.experimental.pallas import tpu as pltpu
from jax.sharding import PartitionSpec as P

CAP = 2
LANES = 128
BLOCK = 256
CHUNKS = 2
HEAD = 2048
STEP = 512
NT = (((1,), (1,)), ((), ()))


def slot_table(ids, probs, experts):
    tok_count = ids.shape[0]
    named = ids.T[None, :, :] == jnp.arange(experts, dtype=jnp.int32)[:, None, None]
    mask = jnp.any(named, axis=1)
    scale = jnp.sum(jnp.where(named, probs.T[None, :, :], 0.0), axis=1)
    order = jnp.arange(tok_count, dtype=jnp.int32)
    before = (order[:, None] < order[None, :])[None, :, :]
    rank = jnp.sum((mask[:, :, None] & before).astype(jnp.int32), axis=1)
    slots = mask[:, None, :] & (rank[:, None, :] == jnp.arange(CAP, dtype=jnp.int32)[None, :, None])
    slot_scale = jnp.sum(jnp.where(slots, scale[:, None, :], 0.0), axis=2)
    return slots.reshape(experts * CAP, tok_count), slot_scale.reshape(experts * CAP)


def head_kernel(me_ref, x_ref, sel_ref, gate_ref, up_ref, out_ref, picked):
    step = pl.program_id(0)
    blocks = pl.num_programs(0) // 4
    group, block = lax.rem(step // blocks + 4 - me_ref[0], 4), step % blocks
    x = x_ref[...].reshape(-1, x_ref.shape[3])
    rows = jnp.dot(sel_ref[0], x, preferred_element_type=jnp.float32).astype(jnp.bfloat16)
    part = rows.shape[0] // 4
    for slot in range(4):
        at = pl.multiple_of(group * (blocks * part * CAP) + (slot % CAP) * (blocks * part) + block * part, 16)
        picked[slot // CAP, pl.ds(at, part), :] = rows[slot * part : (slot + 1) * part]

    @pl.when(step == pl.num_programs(0) - 1)
    def _():
        units = gate_ref.shape[2]
        for e in range(2):
            out_ref[e, :, :units] = jnp.dot(picked[e], gate_ref[e], preferred_element_type=jnp.float32)
            out_ref[e, :, units:] = jnp.dot(picked[e], up_ref[e], preferred_element_type=jnp.float32)


def head_products(me, x_all, sel, w_gate, w_up):
    columns, groups, tok_count, head = x_all.shape
    local_experts, _, units = w_gate.shape
    steps, part, block = sel.shape
    rows = columns * groups * CAP
    blocks = steps // groups
    w_spec = pl.BlockSpec((local_experts, head, units), lambda i, me: (0, 0, 0))
    return pl.pallas_call(
        head_kernel,
        out_shape=jax.ShapeDtypeStruct((local_experts, rows, 2 * units), jnp.float32),
        grid_spec=pltpu.PrefetchScalarGridSpec(
            num_scalar_prefetch=1,
            grid=(steps,),
            in_specs=[
                pl.BlockSpec((columns // blocks, 1, tok_count, head), lambda i, me: (i % blocks, i // blocks, 0, 0)),
                pl.BlockSpec((1, part, block), lambda i, me: (i, 0, 0)),
                w_spec,
                w_spec,
            ],
            out_specs=pl.BlockSpec((local_experts, rows, 2 * units), lambda i, me: (0, 0, 0)),
            scratch_shapes=[pltpu.VMEM((local_experts, rows, head), jnp.bfloat16)],
        ),
        compiler_params=pltpu.CompilerParams(dimension_semantics=("arbitrary",)),
        cost_estimate=pl.CostEstimate(
            flops=2 * local_experts * rows * 2 * units * head + 2 * steps * part * block * head,
            bytes_accessed=25 << 20,
            transcendentals=0,
        ),
        name="head_products",
    )(me, x_all, sel, w_gate, w_up)


def late_kernel(first, own_ref, right_ref, far_ref, left_ref, head_ref, down_ref, gate_ref, up_ref, out_ref, hidden, pre):
    step = pl.program_id(0)
    units = gate_ref.shape[2]

    @pl.when(step == 0)
    def _():
        hidden[...] = jnp.zeros_like(hidden)
        pre[...] = head_ref[0]

    rows = jnp.concatenate([own_ref[...], right_ref[...], far_ref[...], left_ref[...]], axis=0)

    @pl.when(step < first)
    def _():
        hidden[...] += lax.dot_general(rows, down_ref[0], NT, preferred_element_type=jnp.float32)

    @pl.when(step >= first)
    def _():
        pre[:, :units] += jnp.dot(rows, gate_ref[0], preferred_element_type=jnp.float32)
        pre[:, units:] += jnp.dot(rows, up_ref[0], preferred_element_type=jnp.float32)

    @pl.when(step == pl.num_programs(0) - 1)
    def _():
        gate_pre, up_pre, grad = pre[:, :units], pre[:, units:], hidden[...]
        s = jax.nn.sigmoid(gate_pre)
        out_ref[:, :units] = (grad * up_pre * s * (1.0 + gate_pre * (1.0 - s))).astype(jnp.bfloat16)
        out_ref[:, units:] = (grad * gate_pre * s).astype(jnp.bfloat16)


def late_grads(e, own, right, far, left, head_pre, w_down, w_gate, w_up, head):
    _, width, units = w_gate.shape
    rows = 4 * own.shape[0]
    first, steps, skip = width // STEP, (2 * width - head) // STEP, head // STEP
    slot_spec = pl.BlockSpec((own.shape[0], STEP), lambda k: (0, k))
    w_spec = pl.BlockSpec((1, STEP, units), lambda k: (e, skip + jnp.maximum(k - first, 0), 0))
    return pl.pallas_call(
        lambda *refs: late_kernel(first, *refs),
        out_shape=jax.ShapeDtypeStruct((rows, 2 * units), jnp.bfloat16),
        grid=(steps,),
        in_specs=[
            slot_spec,
            slot_spec,
            slot_spec,
            slot_spec,
            pl.BlockSpec((1, rows, 2 * units), lambda k: (e, 0, 0)),
            pl.BlockSpec((1, units, STEP), lambda k: (e, 0, jnp.minimum(k, first - 1))),
            w_spec,
            w_spec,
        ],
        out_specs=pl.BlockSpec((rows, 2 * units), lambda k: (0, 0)),
        scratch_shapes=[pltpu.VMEM((rows, units), jnp.float32), pltpu.VMEM((rows, 2 * units), jnp.float32)],
        compiler_params=pltpu.CompilerParams(dimension_semantics=("arbitrary",)),
        cost_estimate=pl.CostEstimate(
            flops=2 * rows * units * (3 * width - 2 * head), bytes_accessed=10 << 20, transcendentals=rows * units
        ),
        name="late_grads",
    )(own, right, far, left, head_pre, w_down, w_gate, w_up)


def out_kernel(me_ref, h0_ref, h1_ref, gate_ref, up_ref, out_ref):
    units = gate_ref.shape[2]
    for e, h_ref in enumerate((h0_ref, h1_ref)):
        value = lax.dot_general(h_ref[:, :units], gate_ref[e], NT, preferred_element_type=jnp.float32)
        value = value + lax.dot_general(h_ref[:, units:], up_ref[e], NT, preferred_element_type=jnp.float32)
        value = value.astype(jnp.bfloat16)
        part = value.shape[0] // 4
        for r in range(4):
            out_ref[lax.rem(me_ref[0] + r, 4), e * part : (e + 1) * part, :] = value[r * part : (r + 1) * part]


def out_rows(me, h, w_gate, w_up, chunk, chunks, cols):
    rows = h[0].shape[0]
    local_experts, width, units = w_gate.shape
    h_spec = pl.BlockSpec((rows, 2 * units), lambda n, me: (0, 0))
    per = width // chunks // cols
    first = chunk * per
    w_spec = pl.BlockSpec((local_experts, cols, units), lambda n, me: (0, first + n, 0))
    return pl.pallas_call(
        out_kernel,
        out_shape=jax.ShapeDtypeStruct((4, local_experts * rows // 4, width // chunks), jnp.bfloat16),
        grid_spec=pltpu.PrefetchScalarGridSpec(
            num_scalar_prefetch=1,
            grid=(per,),
            in_specs=[
                h_spec,
                h_spec,
                w_spec,
                w_spec,
            ],
            out_specs=pl.BlockSpec((4, local_experts * rows // 4, cols), lambda n, me: (0, 0, n)),
        ),
        compiler_params=pltpu.CompilerParams(dimension_semantics=("arbitrary",)),
        cost_estimate=pl.CostEstimate(
            flops=2 * local_experts * rows * 2 * units * width // chunks, bytes_accessed=8 << 20, transcendentals=0
        ),
        name="out_rows",
    )(me, *h, w_gate, w_up)


def on_device(tokens, out_grad, route_ids, route_probs, w_gate, w_up, w_down):
    columns = lax.axis_size("expert")
    local_experts = w_gate.shape[0]
    experts = local_experts * columns
    tok_count, width = tokens.shape
    slots = experts * CAP
    per_dest = local_experts * CAP
    me = lax.axis_index("dp").astype(jnp.int32).reshape(1)

    with jax.named_scope("gather_tokens"):
        near = lax.all_gather(tokens[:, :HEAD], "dp", axis=0, tiled=True)
        x_all = lax.all_gather(near, "expert", axis=0, tiled=True).reshape(columns, 4, tok_count, HEAD)

    with jax.named_scope("build_slots"):
        table, slot_scale = slot_table(route_ids, route_probs, experts)
        select = table.astype(jnp.bfloat16)
        which = jnp.sum(jnp.where(table, jnp.arange(1, tok_count + 1, dtype=jnp.int32)[None, :], 0), axis=1) - 1
        tag = which.astype(jnp.bfloat16).reshape(columns, local_experts, CAP)
        tiles = []
        for e in range(2):
            choose = select.reshape(columns, local_experts, CAP, tok_count)[:, e].reshape(columns * CAP, tok_count)
            scale = slot_scale.reshape(columns, local_experts, CAP)[:, e].reshape(columns * CAP, 1)
            g_rows = (jnp.dot(choose, out_grad, preferred_element_type=jnp.float32) * scale).astype(jnp.bfloat16)
            x_rows = jnp.dot(choose, tokens[:, HEAD:], preferred_element_type=jnp.float32).astype(jnp.bfloat16)
            parts = [g_rows, x_rows]
            if e == 0:
                both = jnp.broadcast_to(tag.transpose(0, 2, 1)[:, :, :, None], (columns, CAP, 2, LANES // 2))
                parts.append(both.reshape(columns * CAP, LANES))
            tiles.append(jnp.concatenate(parts, axis=1).reshape(columns, CAP, -1))

    up_ring = [(i, (i + 1) % 4) for i in range(4)]
    down_ring = [(i, (i + 3) % 4) for i in range(4)]
    sent = 2 * width - HEAD
    half = columns * CAP

    def send(tile):
        return lax.all_to_all(tile, "expert", split_axis=0, concat_axis=0, tiled=True)

    def by_slot(got):
        return got.transpose(1, 0, 2).reshape(half, -1)

    with jax.named_scope("send_first"):
        got = by_slot(send(tiles[0]))
        a, own_tags = got[:, :sent], got[:, sent:]
        own_tags = own_tags.reshape(CAP, columns, 2, LANES // 2)[:, :, :, 0].transpose(2, 0, 1)
        tags = lax.all_gather(own_tags.reshape(2, half), "dp", axis=0, tiled=True)
    with jax.named_scope("ring_first"):
        left_a = lax.ppermute(a, "dp", up_ring)
        right_a = lax.ppermute(a, "dp", down_ring)
    with jax.named_scope("send_second"):
        second, _ = lax.optimization_barrier((tiles[1], a))
        got, left_a, right_a = lax.optimization_barrier((send(second), left_a, right_a))
        b = by_slot(got)
    with jax.named_scope("ring_far"):
        far_a = lax.ppermute(left_a, "dp", up_ring)
    with jax.named_scope("ring_second"):
        right_b = lax.ppermute(b, "dp", down_ring)
        left_b = lax.ppermute(b, "dp", up_ring)
        far_b = lax.ppermute(right_b, "dp", down_ring)

    with jax.named_scope("token_choice"):
        sources = BLOCK // tok_count
        blocks = columns // sources
        tags = tags.reshape(4, per_dest, blocks, sources).transpose(0, 2, 1, 3)
        target = tags.astype(jnp.int32) + jnp.where(
            tags < 0, -BLOCK, tok_count * jnp.arange(sources, dtype=jnp.int32)
        )
        target = target.reshape(4 * blocks, per_dest * sources)
        sel = (target[:, :, None] == jnp.arange(BLOCK, dtype=jnp.int32)).astype(jnp.bfloat16)

    head_pre = head_products(me, x_all, sel, w_gate, w_up)
    h = (
        late_grads(0, a, right_a, far_a, left_a, head_pre, w_down, w_gate, w_up, HEAD),
        late_grads(1, b, right_b, far_b, left_b, head_pre, w_down, w_gate, w_up, HEAD),
    )

    results = []
    for chunk in range(CHUNKS):
        cols = width // CHUNKS
        partials = out_rows(me, h, w_gate, w_up, chunk, CHUNKS, 256)
        with jax.named_scope("sum_blocks"):
            summed = lax.psum_scatter(
                partials.reshape(4 * slots, cols), "dp", scatter_dimension=0, tiled=True
            )
        with jax.named_scope("return_slots"):
            back = summed.reshape(per_dest, columns, cols).transpose(1, 0, 2)
            returned = lax.all_to_all(back, "expert", split_axis=0, concat_axis=0, tiled=True)
        with jax.named_scope("combine"):
            results.append(
                lax.dot_general(
                    select, returned.reshape(slots, cols), (((0,), (0,)), ((), ())),
                    preferred_element_type=jnp.float32,
                ).astype(jnp.bfloat16)
            )
    return jnp.concatenate(results, axis=1)


def solution(mesh):
    placed = (
        P(("dp", "expert"), None),
        P(("dp", "expert"), None),
        P(("dp", "expert"), None),
        P(("dp", "expert"), None),
        P("expert", None, "dp"),
        P("expert", None, "dp"),
        P("expert", "dp", None),
    )
    return jax.shard_map(
        on_device, mesh=mesh, in_specs=placed, out_specs=P(("dp", "expert"), None), check_vma=False
    )
```

```python
import jax
import jax.numpy as jnp
from jax import lax
from jax.experimental import pallas as pl
from jax.experimental.pallas import tpu as pltpu
from jax.sharding import PartitionSpec as P

CAP = 2
LANES = 128
BLOCK = 256
CHUNKS = 2
HEAD = 1792
STEP = 512
TAIL_STEP = 256
NT = (((1,), (1,)), ((), ()))


def slot_table(ids, probs, experts):
    tok_count = ids.shape[0]
    named = ids.T[None, :, :] == jnp.arange(experts, dtype=jnp.int32)[:, None, None]
    mask = jnp.any(named, axis=1)
    scale = jnp.sum(jnp.where(named, probs.T[None, :, :], 0.0), axis=1)
    order = jnp.arange(tok_count, dtype=jnp.int32)
    before = (order[:, None] < order[None, :])[None, :, :]
    rank = jnp.sum((mask[:, :, None] & before).astype(jnp.int32), axis=1)
    slots = mask[:, None, :] & (rank[:, None, :] == jnp.arange(CAP, dtype=jnp.int32)[None, :, None])
    slot_scale = jnp.sum(jnp.where(slots, scale[:, None, :], 0.0), axis=2)
    return slots.reshape(experts * CAP, tok_count), slot_scale.reshape(experts * CAP)


def head_kernel(first_ref, x_ref, gate_ref, up_ref, out_ref, picked):
    group = pl.program_id(0)
    head = gate_ref.shape[1]
    columns, _, tok_count, _ = x_ref.shape
    sources = BLOCK // tok_count
    from_tok = lax.broadcasted_iota(jnp.int32, (BLOCK, BLOCK), 0)
    to_tok = lax.broadcasted_iota(jnp.int32, (BLOCK, BLOCK), 1)
    earlier = ((from_tok // tok_count == to_tok // tok_count) & (from_tok < to_tok)).astype(jnp.bfloat16)
    ones = jnp.ones((sources, LANES), jnp.bfloat16)
    mine = lax.broadcasted_iota(jnp.int32, (sources, BLOCK), 0) == (
        lax.broadcasted_iota(jnp.int32, (sources, BLOCK), 1) // tok_count
    )
    for block in range(columns // sources):
        part = pl.ds(block * sources, sources)
        ids = x_ref[part, :, :, head:].reshape(BLOCK, LANES).astype(jnp.float32)
        picks = []
        for e in range(2):
            named = (ids == (first_ref[0] + e).astype(jnp.float32)).astype(jnp.bfloat16)
            mask = lax.dot_general(ones, named, NT, preferred_element_type=jnp.float32)
            rank = jnp.dot(mask.astype(jnp.bfloat16), earlier, preferred_element_type=jnp.float32)
            for c in range(CAP):
                chosen = mine & (mask > 0.5) & (jnp.abs(rank - c) < 0.5)
                picks.append(jnp.where(chosen, 1.0, 0.0).astype(jnp.bfloat16))
        x = x_ref[part, :, :, :head].reshape(BLOCK, head)
        rows = jnp.dot(jnp.concatenate(picks, axis=0), x, preferred_element_type=jnp.float32).astype(jnp.bfloat16)
        for slot in range(4):
            at = pl.multiple_of((group * CAP + slot % CAP) * columns + block * sources, 16)
            picked[slot // CAP, pl.ds(at, sources), :] = rows[slot * sources : (slot + 1) * sources]

    @pl.when(group == pl.num_programs(0) - 1)
    def _():
        units = gate_ref.shape[2]
        for e in range(2):
            out_ref[e, :, :units] = jnp.dot(picked[e], gate_ref[e], preferred_element_type=jnp.float32)
            out_ref[e, :, units:] = jnp.dot(picked[e], up_ref[e], preferred_element_type=jnp.float32)


def head_products(first, x_all, w_gate, w_up):
    columns, groups, tok_count, wide = x_all.shape
    head = wide - LANES
    local_experts, _, units = w_gate.shape
    rows = columns * groups * CAP
    w_spec = pl.BlockSpec((local_experts, head, units), lambda i, first: (0, 0, 0))
    return pl.pallas_call(
        head_kernel,
        out_shape=jax.ShapeDtypeStruct((local_experts, rows, 2 * units), jnp.float32),
        grid_spec=pltpu.PrefetchScalarGridSpec(
            num_scalar_prefetch=1,
            grid=(groups,),
            in_specs=[
                pl.BlockSpec((columns, 1, tok_count, wide), lambda i, first: (0, i, 0, 0)),
                w_spec,
                w_spec,
            ],
            out_specs=pl.BlockSpec((local_experts, rows, 2 * units), lambda i, first: (0, 0, 0)),
            scratch_shapes=[pltpu.VMEM((local_experts, rows, head), jnp.bfloat16)],
        ),
        compiler_params=pltpu.CompilerParams(dimension_semantics=("arbitrary",)),
        cost_estimate=pl.CostEstimate(
            flops=2 * local_experts * rows * 2 * units * head + rows * BLOCK * head,
            bytes_accessed=20 << 20,
            transcendentals=0,
        ),
        name="head_products",
    )(first, x_all, w_gate, w_up)


def hidden_kernel(own_ref, right_ref, far_ref, left_ref, down_ref, out_ref):
    @pl.when(pl.program_id(0) == 0)
    def _():
        out_ref[...] = jnp.zeros_like(out_ref)

    rows = jnp.concatenate([own_ref[...], right_ref[...], far_ref[...], left_ref[...]], axis=0)
    out_ref[...] += lax.dot_general(rows, down_ref[0], NT, preferred_element_type=jnp.float32)


def hidden_grads(e, parts, w_down):
    _, units, _ = w_down.shape
    count, wide = parts[0].shape
    slot_spec = pl.BlockSpec((count, STEP), lambda k: (0, k))
    return pl.pallas_call(
        hidden_kernel,
        out_shape=jax.ShapeDtypeStruct((4 * count, units), jnp.float32),
        grid=(wide // STEP,),
        in_specs=[slot_spec] * 4 + [pl.BlockSpec((1, units, STEP), lambda k: (e, 0, k))],
        out_specs=pl.BlockSpec((4 * count, units), lambda k: (0, 0)),
        compiler_params=pltpu.CompilerParams(dimension_semantics=("arbitrary",)),
        cost_estimate=pl.CostEstimate(flops=8 * count * units * wide, bytes_accessed=5 << 20, transcendentals=0),
        name="hidden_grads",
    )(*parts, w_down)


def late_kernel(own_ref, right_ref, far_ref, left_ref, hidden_ref, head_ref, gate_ref, up_ref, out_ref, pre):
    step = pl.program_id(0)
    units = gate_ref.shape[2]

    @pl.when(step == 0)
    def _():
        pre[...] = head_ref[0]

    rows = jnp.concatenate([own_ref[...], right_ref[...], far_ref[...], left_ref[...]], axis=0)
    pre[:, :units] += jnp.dot(rows, gate_ref[0], preferred_element_type=jnp.float32)
    pre[:, units:] += jnp.dot(rows, up_ref[0], preferred_element_type=jnp.float32)

    @pl.when(step == pl.num_programs(0) - 1)
    def _():
        gate_pre, up_pre, grad = pre[:, :units], pre[:, units:], hidden_ref[...]
        s = jax.nn.sigmoid(gate_pre)
        out_ref[:, :units] = (grad * up_pre * s * (1.0 + gate_pre * (1.0 - s))).astype(jnp.bfloat16)
        out_ref[:, units:] = (grad * gate_pre * s).astype(jnp.bfloat16)


def late_grads(e, parts, hidden, head_pre, w_gate, w_up):
    _, width, units = w_gate.shape
    count, wide = parts[0].shape
    rows = 4 * count
    slot_spec = pl.BlockSpec((count, TAIL_STEP), lambda k: (0, k))
    w_spec = pl.BlockSpec((1, TAIL_STEP, units), lambda k: (e, HEAD // TAIL_STEP + k, 0))
    return pl.pallas_call(
        late_kernel,
        out_shape=jax.ShapeDtypeStruct((rows, 2 * units), jnp.bfloat16),
        grid=(wide // TAIL_STEP,),
        in_specs=[slot_spec] * 4
        + [
            pl.BlockSpec((rows, units), lambda k: (0, 0)),
            pl.BlockSpec((1, rows, 2 * units), lambda k: (e, 0, 0)),
            w_spec,
            w_spec,
        ],
        out_specs=pl.BlockSpec((rows, 2 * units), lambda k: (0, 0)),
        scratch_shapes=[pltpu.VMEM((rows, 2 * units), jnp.float32)],
        compiler_params=pltpu.CompilerParams(dimension_semantics=("arbitrary",)),
        cost_estimate=pl.CostEstimate(
            flops=4 * rows * units * wide, bytes_accessed=6 << 20, transcendentals=rows * units
        ),
        name="late_grads",
    )(*parts, hidden, head_pre, w_gate, w_up)


def out_kernel(me_ref, h0_ref, h1_ref, gate_ref, up_ref, out_ref):
    units = gate_ref.shape[2]
    for e, h_ref in enumerate((h0_ref, h1_ref)):
        value = lax.dot_general(h_ref[:, :units], gate_ref[e], NT, preferred_element_type=jnp.float32)
        value = value + lax.dot_general(h_ref[:, units:], up_ref[e], NT, preferred_element_type=jnp.float32)
        value = value.astype(jnp.bfloat16)
        part = value.shape[0] // 4
        for r in range(4):
            out_ref[lax.rem(me_ref[0] + r, 4), e * part : (e + 1) * part, :] = value[r * part : (r + 1) * part]


def out_rows(me, h, w_gate, w_up, chunk, chunks, cols):
    rows = h[0].shape[0]
    local_experts, width, units = w_gate.shape
    h_spec = pl.BlockSpec((rows, 2 * units), lambda n, me: (0, 0))
    per = width // chunks // cols
    first = chunk * per
    w_spec = pl.BlockSpec((local_experts, cols, units), lambda n, me: (0, first + n, 0))
    return pl.pallas_call(
        out_kernel,
        out_shape=jax.ShapeDtypeStruct((4, local_experts * rows // 4, width // chunks), jnp.bfloat16),
        grid_spec=pltpu.PrefetchScalarGridSpec(
            num_scalar_prefetch=1,
            grid=(per,),
            in_specs=[
                h_spec,
                h_spec,
                w_spec,
                w_spec,
            ],
            out_specs=pl.BlockSpec((4, local_experts * rows // 4, cols), lambda n, me: (0, 0, n)),
        ),
        compiler_params=pltpu.CompilerParams(dimension_semantics=("arbitrary",)),
        cost_estimate=pl.CostEstimate(
            flops=2 * local_experts * rows * 2 * units * width // chunks, bytes_accessed=8 << 20, transcendentals=0
        ),
        name="out_rows",
    )(me, *h, w_gate, w_up)


def on_device(tokens, out_grad, route_ids, route_probs, w_gate, w_up, w_down):
    columns = lax.axis_size("expert")
    local_experts = w_gate.shape[0]
    experts = local_experts * columns
    tok_count, width = tokens.shape
    slots = experts * CAP
    per_dest = local_experts * CAP
    me = lax.axis_index("dp").astype(jnp.int32).reshape(1)
    first = (lax.axis_index("expert").astype(jnp.int32) * local_experts).reshape(1)

    up_ring = [(i, (i + 1) % 4) for i in range(4)]
    down_ring = [(i, (i + 3) % 4) for i in range(4)]
    far_ring = [(i, (i + 2) % 4) for i in range(4)]

    def forward(parts, upward):
        return lax.ppermute(parts[3], "dp", up_ring) if upward else lax.ppermute(parts[1], "dp", down_ring)

    with jax.named_scope("gather_tokens"):
        ids = jnp.pad(route_ids.astype(jnp.bfloat16), ((0, 0), (0, LANES - route_ids.shape[1])), constant_values=-1)
        mine = jnp.concatenate([tokens[:, :HEAD], ids], axis=1)
        near = jnp.concatenate([mine] + [lax.ppermute(mine, "dp", ring) for ring in (down_ring, far_ring, up_ring)])
        x_all = lax.all_gather(near, "expert", axis=0, tiled=True).reshape(columns, 4, tok_count, HEAD + LANES)

    with jax.named_scope("build_slots"):
        table, slot_scale = slot_table(route_ids, route_probs, experts)
        select = table.astype(jnp.bfloat16)
        tiles = {}
        for e in range(2):
            choose = select.reshape(columns, local_experts, CAP, tok_count)[:, e].reshape(columns * CAP, tok_count)
            scale = slot_scale.reshape(columns, local_experts, CAP)[:, e].reshape(columns * CAP, 1)
            g_rows = jnp.dot(choose, out_grad, preferred_element_type=jnp.float32) * scale
            x_rows = jnp.dot(choose, tokens[:, HEAD:], preferred_element_type=jnp.float32)
            tiles["g", e] = g_rows.astype(jnp.bfloat16).reshape(columns, CAP, -1)
            tiles["x", e] = x_rows.astype(jnp.bfloat16).reshape(columns, CAP, -1)

    order = (("x", 0), ("g", 0), ("g", 1), ("x", 1))
    upward = (False, True, False, True)
    sent = {}
    for n, name in enumerate(order):
        tile = tiles[name]
        last = sent[order[n - 1]] if n else None
        with jax.named_scope("send_slots"):
            if n:
                tile, _ = lax.optimization_barrier((tile, last[0]))
            got = lax.all_to_all(tile, "expert", split_axis=0, concat_axis=0, tiled=True)
            if n == len(order) - 1:
                head_pre = head_products(first, x_all, w_gate, w_up)
                got, last[1], last[3], head_pre = lax.optimization_barrier((got, last[1], last[3], head_pre))
            elif n == 2:
                early = sent[order[0]]
                got, last[1], last[3], early[2] = lax.optimization_barrier((got, last[1], last[3], early[2]))
            elif n:
                got, last[1], last[3] = lax.optimization_barrier((got, last[1], last[3]))
            own = got.transpose(1, 0, 2).reshape(columns * CAP, -1)
        with jax.named_scope("ring"):
            if n:
                last[2] = forward(last, upward[n - 1])
            right = lax.ppermute(own, "dp", down_ring)
            left = lax.ppermute(own, "dp", up_ring)
            sent[name] = [own, right, None, left]

    hidden = hidden_grads(0, sent["g", 0], w_down)
    h = [late_grads(0, sent["x", 0], hidden, head_pre, w_gate, w_up)]
    with jax.named_scope("ring"):
        final = sent["x", 1]
        final[2] = forward(final, upward[3])
    hidden = hidden_grads(1, sent["g", 1], w_down)
    h.append(late_grads(1, final, hidden, head_pre, w_gate, w_up))

    results = []
    for chunk in range(CHUNKS):
        cols = width // CHUNKS
        partials = out_rows(me, h, w_gate, w_up, chunk, CHUNKS, 256)
        with jax.named_scope("sum_blocks"):
            summed = lax.psum_scatter(
                partials.reshape(4 * slots, cols), "dp", scatter_dimension=0, tiled=True
            )
        with jax.named_scope("return_slots"):
            back = summed.reshape(per_dest, columns, cols).transpose(1, 0, 2)
            returned = lax.all_to_all(back, "expert", split_axis=0, concat_axis=0, tiled=True)
        with jax.named_scope("combine"):
            results.append(
                lax.dot_general(
                    select, returned.reshape(slots, cols), (((0,), (0,)), ((), ())),
                    preferred_element_type=jnp.float32,
                ).astype(jnp.bfloat16)
            )
    return jnp.concatenate(results, axis=1)


def solution(mesh):
    placed = (
        P(("dp", "expert"), None),
        P(("dp", "expert"), None),
        P(("dp", "expert"), None),
        P(("dp", "expert"), None),
        P("expert", None, "dp"),
        P("expert", None, "dp"),
        P("expert", "dp", None),
    )
    return jax.shard_map(
        on_device, mesh=mesh, in_specs=placed, out_specs=P(("dp", "expert"), None), check_vma=False
    )
```

```python
import jax
import jax.numpy as jnp
from jax import lax
from jax.experimental import pallas as pl
from jax.experimental.pallas import tpu as pltpu
from jax.sharding import PartitionSpec as P

CAP = 2
LANES = 128
BLOCK = 256
HEAD = 1792
STEP = 1792
TAIL_STEP = 896
OUT_STEP = 512
OUT_SPLIT = 1536
NT = (((1,), (1,)), ((), ()))


def slot_table(ids, probs, experts):
    tok_count = ids.shape[0]
    named = ids.T[None, :, :] == jnp.arange(experts, dtype=jnp.int32)[:, None, None]
    mask = jnp.any(named, axis=1)
    scale = jnp.sum(jnp.where(named, probs.T[None, :, :], 0.0), axis=1)
    order = jnp.arange(tok_count, dtype=jnp.int32)
    before = (order[:, None] < order[None, :])[None, :, :]
    rank = jnp.sum((mask[:, :, None] & before).astype(jnp.int32), axis=1)
    slots = mask[:, None, :] & (rank[:, None, :] == jnp.arange(CAP, dtype=jnp.int32)[None, :, None])
    slot_scale = jnp.sum(jnp.where(slots, scale[:, None, :], 0.0), axis=2)
    return slots.reshape(experts * CAP, tok_count), slot_scale.reshape(experts * CAP)


def head_kernel(first_ref, x_ref, gate_ref, up_ref, out_ref, picked):
    group = pl.program_id(0)
    head = gate_ref.shape[1]
    columns, _, tok_count, _ = x_ref.shape
    sources = BLOCK // tok_count
    from_tok = lax.broadcasted_iota(jnp.int32, (BLOCK, BLOCK), 0)
    to_tok = lax.broadcasted_iota(jnp.int32, (BLOCK, BLOCK), 1)
    earlier = ((from_tok // tok_count == to_tok // tok_count) & (from_tok < to_tok)).astype(jnp.bfloat16)
    ones = jnp.ones((sources, LANES), jnp.bfloat16)
    mine = lax.broadcasted_iota(jnp.int32, (sources, BLOCK), 0) == (
        lax.broadcasted_iota(jnp.int32, (sources, BLOCK), 1) // tok_count
    )
    for block in range(columns // sources):
        part = pl.ds(block * sources, sources)
        ids = x_ref[part, :, :, head:].reshape(BLOCK, LANES).astype(jnp.float32)
        picks = []
        for e in range(2):
            named = (ids == (first_ref[0] + e).astype(jnp.float32)).astype(jnp.bfloat16)
            mask = lax.dot_general(ones, named, NT, preferred_element_type=jnp.float32)
            rank = jnp.dot(mask.astype(jnp.bfloat16), earlier, preferred_element_type=jnp.float32)
            for c in range(CAP):
                chosen = mine & (mask > 0.5) & (jnp.abs(rank - c) < 0.5)
                picks.append(jnp.where(chosen, 1.0, 0.0).astype(jnp.bfloat16))
        x = x_ref[part, :, :, :head].reshape(BLOCK, head)
        rows = jnp.dot(jnp.concatenate(picks, axis=0), x, preferred_element_type=jnp.float32).astype(jnp.bfloat16)
        for slot in range(4):
            at = pl.multiple_of((group * CAP + slot % CAP) * columns + block * sources, 16)
            picked[slot // CAP, pl.ds(at, sources), :] = rows[slot * sources : (slot + 1) * sources]

    @pl.when(group == pl.num_programs(0) - 1)
    def _():
        units = gate_ref.shape[2]
        for e in range(2):
            out_ref[e, :, :units] = jnp.dot(picked[e], gate_ref[e], preferred_element_type=jnp.float32)
            out_ref[e, :, units:] = jnp.dot(picked[e], up_ref[e], preferred_element_type=jnp.float32)


def head_products(first, x_all, w_gate, w_up):
    columns, groups, tok_count, wide = x_all.shape
    head = wide - LANES
    local_experts, _, units = w_gate.shape
    rows = columns * groups * CAP
    w_spec = pl.BlockSpec((local_experts, head, units), lambda i, first: (0, 0, 0))
    return pl.pallas_call(
        head_kernel,
        out_shape=jax.ShapeDtypeStruct((local_experts, rows, 2 * units), jnp.float32),
        grid_spec=pltpu.PrefetchScalarGridSpec(
            num_scalar_prefetch=1,
            grid=(groups,),
            in_specs=[
                pl.BlockSpec((columns, 1, tok_count, wide), lambda i, first: (0, i, 0, 0)),
                w_spec,
                w_spec,
            ],
            out_specs=pl.BlockSpec((local_experts, rows, 2 * units), lambda i, first: (0, 0, 0)),
            scratch_shapes=[pltpu.VMEM((local_experts, rows, head), jnp.bfloat16)],
        ),
        compiler_params=pltpu.CompilerParams(dimension_semantics=("arbitrary",)),
        cost_estimate=pl.CostEstimate(
            flops=2 * local_experts * rows * 2 * units * head + rows * BLOCK * head,
            bytes_accessed=20 << 20,
            transcendentals=0,
        ),
        name="head_products",
    )(first, x_all, w_gate, w_up)


def hidden_kernel(own_ref, right_ref, far_ref, left_ref, down_ref, out_ref):
    @pl.when(pl.program_id(0) == 0)
    def _():
        out_ref[...] = jnp.zeros_like(out_ref)

    rows = jnp.concatenate([own_ref[...], right_ref[...], far_ref[...], left_ref[...]], axis=0)
    out_ref[...] += lax.dot_general(rows, down_ref[0], NT, preferred_element_type=jnp.float32)


def hidden_grads(e, parts, w_down):
    _, units, _ = w_down.shape
    count, wide = parts[0].shape
    slot_spec = pl.BlockSpec((count, STEP), lambda k: (0, k))
    return pl.pallas_call(
        hidden_kernel,
        out_shape=jax.ShapeDtypeStruct((4 * count, units), jnp.float32),
        grid=(wide // STEP,),
        in_specs=[slot_spec] * 4 + [pl.BlockSpec((1, units, STEP), lambda k: (e, 0, k))],
        out_specs=pl.BlockSpec((4 * count, units), lambda k: (0, 0)),
        compiler_params=pltpu.CompilerParams(dimension_semantics=("arbitrary",)),
        cost_estimate=pl.CostEstimate(flops=8 * count * units * wide, bytes_accessed=5 << 20, transcendentals=0),
        name="hidden_grads",
    )(*parts, w_down)


def late_kernel(own_ref, right_ref, far_ref, left_ref, hidden_ref, head_ref, gate_ref, up_ref, out_ref, pre):
    step = pl.program_id(0)
    units = gate_ref.shape[2]

    @pl.when(step == 0)
    def _():
        pre[...] = head_ref[0]

    rows = jnp.concatenate([own_ref[...], right_ref[...], far_ref[...], left_ref[...]], axis=0)
    pre[:, :units] += jnp.dot(rows, gate_ref[0], preferred_element_type=jnp.float32)
    pre[:, units:] += jnp.dot(rows, up_ref[0], preferred_element_type=jnp.float32)

    @pl.when(step == pl.num_programs(0) - 1)
    def _():
        gate_pre, up_pre, grad = pre[:, :units], pre[:, units:], hidden_ref[...]
        s = jax.nn.sigmoid(gate_pre)
        out_ref[:, :units] = (grad * up_pre * s * (1.0 + gate_pre * (1.0 - s))).astype(jnp.bfloat16)
        out_ref[:, units:] = (grad * gate_pre * s).astype(jnp.bfloat16)


def late_grads(e, parts, hidden, head_pre, w_gate, w_up):
    _, width, units = w_gate.shape
    count, wide = parts[0].shape
    rows = 4 * count
    slot_spec = pl.BlockSpec((count, TAIL_STEP), lambda k: (0, k))
    w_spec = pl.BlockSpec((1, TAIL_STEP, units), lambda k: (e, HEAD // TAIL_STEP + k, 0))
    return pl.pallas_call(
        late_kernel,
        out_shape=jax.ShapeDtypeStruct((rows, 2 * units), jnp.bfloat16),
        grid=(wide // TAIL_STEP,),
        in_specs=[slot_spec] * 4
        + [
            pl.BlockSpec((rows, units), lambda k: (0, 0)),
            pl.BlockSpec((1, rows, 2 * units), lambda k: (e, 0, 0)),
            w_spec,
            w_spec,
        ],
        out_specs=pl.BlockSpec((rows, 2 * units), lambda k: (0, 0)),
        scratch_shapes=[pltpu.VMEM((rows, 2 * units), jnp.float32)],
        compiler_params=pltpu.CompilerParams(dimension_semantics=("arbitrary",)),
        cost_estimate=pl.CostEstimate(
            flops=4 * rows * units * wide, bytes_accessed=6 << 20, transcendentals=rows * units
        ),
        name="late_grads",
    )(*parts, hidden, head_pre, w_gate, w_up)


def out_kernel(h0_ref, h1_ref, gate_ref, up_ref, *out_refs):
    units = gate_ref.shape[2]
    for e, h_ref in enumerate((h0_ref, h1_ref)):
        value = lax.dot_general(h_ref[:, :units], gate_ref[e], NT, preferred_element_type=jnp.float32)
        value = value + lax.dot_general(h_ref[:, units:], up_ref[e], NT, preferred_element_type=jnp.float32)
        value = value.astype(jnp.bfloat16)
        part = value.shape[0] // 4
        for r, out_ref in enumerate(out_refs):
            out_ref[e * part : (e + 1) * part, :] = value[r * part : (r + 1) * part]


def out_rows(h, w_gate, w_up, start, stop):
    rows = h[0].shape[0]
    local_experts, width, units = w_gate.shape
    count = local_experts * rows // 4
    h_spec = pl.BlockSpec((rows, 2 * units), lambda n: (0, 0))
    w_spec = pl.BlockSpec((local_experts, OUT_STEP, units), lambda n: (0, start // OUT_STEP + n, 0))
    return pl.pallas_call(
        out_kernel,
        out_shape=[jax.ShapeDtypeStruct((count, stop - start), jnp.bfloat16)] * 4,
        grid=((stop - start) // OUT_STEP,),
        in_specs=[h_spec, h_spec, w_spec, w_spec],
        out_specs=[pl.BlockSpec((count, OUT_STEP), lambda n: (0, n))] * 4,
        compiler_params=pltpu.CompilerParams(dimension_semantics=("arbitrary",)),
        cost_estimate=pl.CostEstimate(
            flops=2 * local_experts * rows * 2 * units * (stop - start), bytes_accessed=8 << 20, transcendentals=0
        ),
        name="out_rows",
    )(*h, w_gate, w_up)


def total(*terms):
    value = terms[0].astype(jnp.float32)
    for term in terms[1:]:
        value = value + term.astype(jnp.float32)
    return value.astype(jnp.bfloat16)


def on_device(tokens, out_grad, route_ids, route_probs, w_gate, w_up, w_down):
    columns = lax.axis_size("expert")
    local_experts = w_gate.shape[0]
    experts = local_experts * columns
    tok_count, width = tokens.shape
    slots = experts * CAP
    per_dest = local_experts * CAP
    first = (lax.axis_index("expert").astype(jnp.int32) * local_experts).reshape(1)

    up_ring = [(i, (i + 1) % 4) for i in range(4)]
    down_ring = [(i, (i + 3) % 4) for i in range(4)]
    far_ring = [(i, (i + 2) % 4) for i in range(4)]

    def forward(parts, upward):
        return lax.ppermute(parts[3], "dp", up_ring) if upward else lax.ppermute(parts[1], "dp", down_ring)

    with jax.named_scope("gather_tokens"):
        ids = jnp.pad(route_ids.astype(jnp.bfloat16), ((0, 0), (0, LANES - route_ids.shape[1])), constant_values=-1)
        mine = jnp.concatenate([tokens[:, :HEAD], ids], axis=1)
        near = jnp.concatenate([mine] + [lax.ppermute(mine, "dp", ring) for ring in (down_ring, far_ring, up_ring)])
        x_all = lax.all_gather(near, "expert", axis=0, tiled=True).reshape(columns, 4, tok_count, HEAD + LANES)

    with jax.named_scope("build_slots"):
        table, slot_scale = slot_table(route_ids, route_probs, experts)
        select = table.astype(jnp.bfloat16)
        tiles = {}
        for e in range(2):
            choose = select.reshape(columns, local_experts, CAP, tok_count)[:, e].reshape(columns * CAP, tok_count)
            scale = slot_scale.reshape(columns, local_experts, CAP)[:, e].reshape(columns * CAP, 1)
            g_rows = jnp.dot(choose, out_grad, preferred_element_type=jnp.float32) * scale
            x_rows = jnp.dot(choose, tokens[:, HEAD:], preferred_element_type=jnp.float32)
            tiles["g", e] = g_rows.astype(jnp.bfloat16).reshape(columns, CAP, -1)
            tiles["x", e] = x_rows.astype(jnp.bfloat16).reshape(columns, CAP, -1)

    order = (("x", 0), ("g", 0), ("g", 1), ("x", 1))
    upward = (False, True, False, True)
    sent = {}
    for n, name in enumerate(order):
        tile = tiles[name]
        last = sent[order[n - 1]] if n else None
        with jax.named_scope("send_slots"):
            if n:
                tile, _ = lax.optimization_barrier((tile, last[0]))
            got = lax.all_to_all(tile, "expert", split_axis=0, concat_axis=0, tiled=True)
            if n == len(order) - 1:
                head_pre = head_products(first, x_all, w_gate, w_up)
                got, last[1], last[3], head_pre = lax.optimization_barrier((got, last[1], last[3], head_pre))
            elif n == 2:
                early = sent[order[0]]
                got, last[1], last[3], early[2] = lax.optimization_barrier((got, last[1], last[3], early[2]))
            elif n:
                got, last[1], last[3] = lax.optimization_barrier((got, last[1], last[3]))
            own = got.transpose(1, 0, 2).reshape(columns * CAP, -1)
        with jax.named_scope("ring"):
            if n:
                last[2] = forward(last, upward[n - 1])
            right = lax.ppermute(own, "dp", down_ring)
            left = lax.ppermute(own, "dp", up_ring)
            sent[name] = [own, right, None, left]

    hidden = hidden_grads(0, sent["g", 0], w_down)
    with jax.named_scope("ring"):
        final = sent["x", 1]
        final[1], final[3], hidden = lax.optimization_barrier((final[1], final[3], hidden))
        final[2] = forward(final, upward[3])
    h = [late_grads(0, sent["x", 0], hidden, head_pre, w_gate, w_up)]
    hidden = hidden_grads(1, sent["g", 1], w_down)
    h.append(late_grads(1, final, hidden, head_pre, w_gate, w_up))

    own_a, right_a, far_a, left_a = out_rows(h, w_gate, w_up, 0, OUT_SPLIT)
    own_b, right_b, far_b, left_b = out_rows(h, w_gate, w_up, OUT_SPLIT, width)
    with jax.named_scope("sum_blocks"):
        from_far = lax.ppermute(far_a, "dp", up_ring)
        from_right_a = lax.ppermute(left_a, "dp", down_ring)
        from_left_a = lax.ppermute(total(right_a, from_far), "dp", up_ring)
        far_b, from_right_a = lax.optimization_barrier((far_b, from_right_a))
        from_far = lax.ppermute(far_b, "dp", down_ring)
        right_b, from_left_a = lax.optimization_barrier((right_b, from_left_a))
        from_left_b = lax.ppermute(right_b, "dp", up_ring)
        left_b = total(left_b, from_far)
        left_b, from_left_a = lax.optimization_barrier((left_b, from_left_a))
        from_right_b = lax.ppermute(left_b, "dp", down_ring)

    results = []
    for terms in ((own_a, from_left_a, from_right_a), (own_b, from_left_b, from_right_b)):
        with jax.named_scope("return_slots"):
            summed = total(*terms)
            cols = summed.shape[1]
            back = summed.reshape(per_dest, columns, cols).transpose(1, 0, 2)
            returned = lax.all_to_all(back, "expert", split_axis=0, concat_axis=0, tiled=True)
        with jax.named_scope("combine"):
            results.append(
                lax.dot_general(
                    select, returned.reshape(slots, cols), (((0,), (0,)), ((), ())),
                    preferred_element_type=jnp.float32,
                ).astype(jnp.bfloat16)
            )
    return jnp.concatenate(results, axis=1)


def solution(mesh):
    placed = (
        P(("dp", "expert"), None),
        P(("dp", "expert"), None),
        P(("dp", "expert"), None),
        P(("dp", "expert"), None),
        P("expert", None, "dp"),
        P("expert", None, "dp"),
        P("expert", "dp", None),
    )
    return jax.shard_map(
        on_device, mesh=mesh, in_specs=placed, out_specs=P(("dp", "expert"), None), check_vma=False
    )
```

```python
import jax
import jax.numpy as jnp
from jax import lax
from jax.experimental import pallas as pl
from jax.experimental.pallas import tpu as pltpu
from jax.sharding import PartitionSpec as P

CAP = 2
LANES = 128
X_SPLIT = 1792
STEP = 896
OUT_STEP = 512
OUT_SPLIT = 1536
NT = (((1,), (1,)), ((), ()))


def slot_table(ids, probs, experts):
    tok_count = ids.shape[0]
    named = ids.T[None, :, :] == jnp.arange(experts, dtype=jnp.int32)[:, None, None]
    mask = jnp.any(named, axis=1)
    scale = jnp.sum(jnp.where(named, probs.T[None, :, :], 0.0), axis=1)
    order = jnp.arange(tok_count, dtype=jnp.int32)
    before = (order[:, None] < order[None, :])[None, :, :]
    rank = jnp.sum((mask[:, :, None] & before).astype(jnp.int32), axis=1)
    slots = mask[:, None, :] & (rank[:, None, :] == jnp.arange(CAP, dtype=jnp.int32)[None, :, None])
    slot_scale = jnp.sum(jnp.where(slots, scale[:, None, :], 0.0), axis=2)
    return slots.reshape(experts * CAP, tok_count), slot_scale.reshape(experts * CAP)


def hidden_kernel(own_ref, right_ref, far_ref, left_ref, down_ref, out_ref):
    @pl.when(pl.program_id(0) == 0)
    def _():
        out_ref[...] = jnp.zeros_like(out_ref)

    rows = jnp.concatenate([own_ref[...], right_ref[...], far_ref[...], left_ref[...]], axis=0)
    out_ref[...] += lax.dot_general(rows, down_ref[0], NT, preferred_element_type=jnp.float32)


def hidden_grads(e, parts, w_down):
    _, units, _ = w_down.shape
    count, wide = parts[0].shape
    slot_spec = pl.BlockSpec((count, STEP), lambda k: (0, k))
    return pl.pallas_call(
        hidden_kernel,
        out_shape=jax.ShapeDtypeStruct((4 * count, units), jnp.float32),
        grid=(wide // STEP,),
        in_specs=[slot_spec] * 4 + [pl.BlockSpec((1, units, STEP), lambda k: (e, 0, k))],
        out_specs=pl.BlockSpec((4 * count, units), lambda k: (0, 0)),
        compiler_params=pltpu.CompilerParams(dimension_semantics=("arbitrary",)),
        cost_estimate=pl.CostEstimate(flops=8 * count * units * wide, bytes_accessed=5 << 20, transcendentals=0),
        name="hidden_grads",
    )(*parts, w_down)


def gate_kernel(own_ref, right_ref, far_ref, left_ref, gate_ref, up_ref, out_ref):
    units = gate_ref.shape[2]
    rows = jnp.concatenate([own_ref[...], right_ref[...], far_ref[...], left_ref[...]], axis=0)

    @pl.when(pl.program_id(0) == 0)
    def _():
        out_ref[...] = jnp.zeros_like(out_ref)

    out_ref[:, :units] += jnp.dot(rows, gate_ref[0], preferred_element_type=jnp.float32)
    out_ref[:, units:] += jnp.dot(rows, up_ref[0], preferred_element_type=jnp.float32)


def gate_products(e, parts, w_gate, w_up):
    units = w_gate.shape[2]
    count, wide = parts[0].shape
    slot_spec = pl.BlockSpec((count, STEP), lambda k: (0, k))
    w_spec = pl.BlockSpec((1, STEP, units), lambda k: (e, k, 0))
    return pl.pallas_call(
        gate_kernel,
        out_shape=jax.ShapeDtypeStruct((4 * count, 2 * units), jnp.float32),
        grid=(wide // STEP,),
        in_specs=[slot_spec] * 4 + [w_spec, w_spec],
        out_specs=pl.BlockSpec((4 * count, 2 * units), lambda k: (0, 0)),
        compiler_params=pltpu.CompilerParams(dimension_semantics=("arbitrary",)),
        cost_estimate=pl.CostEstimate(flops=16 * count * units * wide, bytes_accessed=5 << 20, transcendentals=0),
        name="gate_products",
    )(*parts, w_gate, w_up)


def late_kernel(own_ref, right_ref, far_ref, left_ref, hidden_ref, pre_ref, gate_ref, up_ref, out_ref, pre):
    step = pl.program_id(0)
    units = gate_ref.shape[2]

    @pl.when(step == 0)
    def _():
        pre[...] = pre_ref[...]

    rows = jnp.concatenate([own_ref[...], right_ref[...], far_ref[...], left_ref[...]], axis=0)
    pre[:, :units] += jnp.dot(rows, gate_ref[0], preferred_element_type=jnp.float32)
    pre[:, units:] += jnp.dot(rows, up_ref[0], preferred_element_type=jnp.float32)

    @pl.when(step == pl.num_programs(0) - 1)
    def _():
        gate_pre, up_pre, grad = pre[:, :units], pre[:, units:], hidden_ref[...]
        s = jax.nn.sigmoid(gate_pre)
        out_ref[:, :units] = (grad * up_pre * s * (1.0 + gate_pre * (1.0 - s))).astype(jnp.bfloat16)
        out_ref[:, units:] = (grad * gate_pre * s).astype(jnp.bfloat16)


def late_grads(e, parts, hidden, pre, w_gate, w_up):
    units = w_gate.shape[2]
    count, wide = parts[0].shape
    rows = 4 * count
    slot_spec = pl.BlockSpec((count, STEP), lambda k: (0, k))
    w_spec = pl.BlockSpec((1, STEP, units), lambda k: (e, X_SPLIT // STEP + k, 0))
    return pl.pallas_call(
        late_kernel,
        out_shape=jax.ShapeDtypeStruct((rows, 2 * units), jnp.bfloat16),
        grid=(wide // STEP,),
        in_specs=[slot_spec] * 4
        + [
            pl.BlockSpec((rows, units), lambda k: (0, 0)),
            pl.BlockSpec((rows, 2 * units), lambda k: (0, 0)),
            w_spec,
            w_spec,
        ],
        out_specs=pl.BlockSpec((rows, 2 * units), lambda k: (0, 0)),
        scratch_shapes=[pltpu.VMEM((rows, 2 * units), jnp.float32)],
        compiler_params=pltpu.CompilerParams(dimension_semantics=("arbitrary",)),
        cost_estimate=pl.CostEstimate(
            flops=4 * rows * units * wide, bytes_accessed=6 << 20, transcendentals=rows * units
        ),
        name="late_grads",
    )(*parts, hidden, pre, w_gate, w_up)


def out_kernel(h0_ref, h1_ref, gate_ref, up_ref, *out_refs):
    units = gate_ref.shape[2]
    for e, h_ref in enumerate((h0_ref, h1_ref)):
        value = lax.dot_general(h_ref[:, :units], gate_ref[e], NT, preferred_element_type=jnp.float32)
        value = value + lax.dot_general(h_ref[:, units:], up_ref[e], NT, preferred_element_type=jnp.float32)
        value = value.astype(jnp.bfloat16)
        part = value.shape[0] // 4
        for r, out_ref in enumerate(out_refs):
            out_ref[e * part : (e + 1) * part, :] = value[r * part : (r + 1) * part]


def out_rows(h, w_gate, w_up, start, stop):
    rows = h[0].shape[0]
    local_experts, width, units = w_gate.shape
    count = local_experts * rows // 4
    h_spec = pl.BlockSpec((rows, 2 * units), lambda n: (0, 0))
    w_spec = pl.BlockSpec((local_experts, OUT_STEP, units), lambda n: (0, start // OUT_STEP + n, 0))
    return pl.pallas_call(
        out_kernel,
        out_shape=[jax.ShapeDtypeStruct((count, stop - start), jnp.bfloat16)] * 4,
        grid=((stop - start) // OUT_STEP,),
        in_specs=[h_spec, h_spec, w_spec, w_spec],
        out_specs=[pl.BlockSpec((count, OUT_STEP), lambda n: (0, n))] * 4,
        compiler_params=pltpu.CompilerParams(dimension_semantics=("arbitrary",)),
        cost_estimate=pl.CostEstimate(
            flops=2 * local_experts * rows * 2 * units * (stop - start), bytes_accessed=8 << 20, transcendentals=0
        ),
        name="out_rows",
    )(*h, w_gate, w_up)


def total(*terms):
    value = terms[0].astype(jnp.float32)
    for term in terms[1:]:
        value = value + term.astype(jnp.float32)
    return value.astype(jnp.bfloat16)


def on_device(tokens, out_grad, route_ids, route_probs, w_gate, w_up, w_down):
    columns = lax.axis_size("expert")
    local_experts = w_gate.shape[0]
    experts = local_experts * columns
    tok_count, width = tokens.shape
    slots = experts * CAP
    per_dest = local_experts * CAP
    up_ring = [(i, (i + 1) % 4) for i in range(4)]
    down_ring = [(i, (i + 3) % 4) for i in range(4)]

    with jax.named_scope("build_slots"):
        table, slot_scale = slot_table(route_ids, route_probs, experts)
        select = table.astype(jnp.bfloat16)

        def tile(kind, e):
            choose = select.reshape(columns, local_experts, CAP, tok_count)[:, e].reshape(columns * CAP, tok_count)
            if kind == "g":
                scale = slot_scale.reshape(columns, local_experts, CAP)[:, e].reshape(columns * CAP, 1)
                rows = jnp.dot(choose, out_grad, preferred_element_type=jnp.float32) * scale
            else:
                source = tokens[:, :X_SPLIT] if kind == "x" else tokens[:, X_SPLIT:]
                rows = jnp.dot(choose, source, preferred_element_type=jnp.float32)
            return rows.astype(jnp.bfloat16).reshape(columns, CAP, -1)

    order = (("x", 0), ("y", 0), ("g", 0), ("g", 1), ("x", 1), ("y", 1))
    upward = (True, False, True, False, True, False)
    sent = []
    for n, name in enumerate(order):
        with jax.named_scope("send_slots"):
            slab = tile(*name)
            if n:
                slab, _ = lax.optimization_barrier((slab, sent[-1][0]))
            got = lax.all_to_all(slab, "expert", split_axis=0, concat_axis=0, tiled=True)
            if n:
                last = sent[-1]
                got, last[1], last[3] = lax.optimization_barrier((got, last[1], last[3]))
            if n > 1:
                got, sent[-2][2] = lax.optimization_barrier((got, sent[-2][2]))
            own = got.transpose(1, 0, 2).reshape(columns * CAP, -1)
        with jax.named_scope("ring"):
            right = lax.ppermute(own, "dp", down_ring)
            left = lax.ppermute(own, "dp", up_ring)
            far = lax.ppermute(left, "dp", up_ring) if upward[n] else lax.ppermute(right, "dp", down_ring)
            sent.append([own, right, far, left])
    parts = dict(zip(order, sent))

    h = []
    for e in range(2):
        hidden = hidden_grads(e, parts["g", e], w_down)
        pre = gate_products(e, parts["x", e], w_gate, w_up)
        h.append(late_grads(e, parts["y", e], hidden, pre, w_gate, w_up))

    own_a, right_a, far_a, left_a = out_rows(h, w_gate, w_up, 0, OUT_SPLIT)
    own_b, right_b, far_b, left_b = out_rows(h, w_gate, w_up, OUT_SPLIT, width)
    with jax.named_scope("sum_blocks"):
        from_far = lax.ppermute(far_a, "dp", up_ring)
        from_right_a = lax.ppermute(left_a, "dp", down_ring)
        from_left_a = lax.ppermute(total(right_a, from_far), "dp", up_ring)
        far_b, from_right_a = lax.optimization_barrier((far_b, from_right_a))
        from_far = lax.ppermute(far_b, "dp", down_ring)
        right_b, from_left_a = lax.optimization_barrier((right_b, from_left_a))
        from_left_b = lax.ppermute(right_b, "dp", up_ring)
        left_b = total(left_b, from_far)
        left_b, from_left_a = lax.optimization_barrier((left_b, from_left_a))
        from_right_b = lax.ppermute(left_b, "dp", down_ring)

    results = []
    for terms in ((own_a, from_left_a, from_right_a), (own_b, from_left_b, from_right_b)):
        with jax.named_scope("return_slots"):
            summed = total(*terms)
            cols = summed.shape[1]
            back = summed.reshape(per_dest, columns, cols).transpose(1, 0, 2)
            returned = lax.all_to_all(back, "expert", split_axis=0, concat_axis=0, tiled=True)
        with jax.named_scope("combine"):
            results.append(
                lax.dot_general(
                    select, returned.reshape(slots, cols), (((0,), (0,)), ((), ())),
                    preferred_element_type=jnp.float32,
                ).astype(jnp.bfloat16)
            )
    return jnp.concatenate(results, axis=1)


def solution(mesh):
    placed = (
        P(("dp", "expert"), None),
        P(("dp", "expert"), None),
        P(("dp", "expert"), None),
        P(("dp", "expert"), None),
        P("expert", None, "dp"),
        P("expert", None, "dp"),
        P("expert", "dp", None),
    )
    return jax.shard_map(
        on_device, mesh=mesh, in_specs=placed, out_specs=P(("dp", "expert"), None), check_vma=False
    )
```

```python
import jax
import jax.numpy as jnp
from jax import lax
from jax.experimental import pallas as pl
from jax.experimental.pallas import tpu as pltpu
from jax.sharding import PartitionSpec as P

CAP = 2
LANES = 128
BLOCK = 256
HEAD = 1792
STEP = 1792
TAIL_STEP = 896
OUT_STEP = 512
OUT_SPLIT = 1536
NT = (((1,), (1,)), ((), ()))


def slot_table(ids, probs, experts):
    tok_count = ids.shape[0]
    named = ids.T[None, :, :] == jnp.arange(experts, dtype=jnp.int32)[:, None, None]
    mask = jnp.any(named, axis=1)
    scale = jnp.sum(jnp.where(named, probs.T[None, :, :], 0.0), axis=1)
    order = jnp.arange(tok_count, dtype=jnp.int32)
    before = (order[:, None] < order[None, :])[None, :, :]
    rank = jnp.sum((mask[:, :, None] & before).astype(jnp.int32), axis=1)
    slots = mask[:, None, :] & (rank[:, None, :] == jnp.arange(CAP, dtype=jnp.int32)[None, :, None])
    slot_scale = jnp.sum(jnp.where(slots, scale[:, None, :], 0.0), axis=2)
    return slots.reshape(experts * CAP, tok_count), slot_scale.reshape(experts * CAP)


def head_kernel(first_ref, x_ref, gate_ref, up_ref, out_ref, picked):
    group = pl.program_id(0)
    head = gate_ref.shape[1]
    columns, _, tok_count, _ = x_ref.shape
    sources = BLOCK // tok_count
    from_tok = lax.broadcasted_iota(jnp.int32, (BLOCK, BLOCK), 0)
    to_tok = lax.broadcasted_iota(jnp.int32, (BLOCK, BLOCK), 1)
    earlier = ((from_tok // tok_count == to_tok // tok_count) & (from_tok < to_tok)).astype(jnp.bfloat16)
    ones = jnp.ones((sources, LANES), jnp.bfloat16)
    mine = lax.broadcasted_iota(jnp.int32, (sources, BLOCK), 0) == (
        lax.broadcasted_iota(jnp.int32, (sources, BLOCK), 1) // tok_count
    )
    for block in range(columns // sources):
        part = pl.ds(block * sources, sources)
        ids = x_ref[part, :, :, head:].reshape(BLOCK, LANES).astype(jnp.float32)
        picks = []
        for e in range(2):
            named = (ids == (first_ref[0] + e).astype(jnp.float32)).astype(jnp.bfloat16)
            mask = lax.dot_general(ones, named, NT, preferred_element_type=jnp.float32)
            rank = jnp.dot(mask.astype(jnp.bfloat16), earlier, preferred_element_type=jnp.float32)
            for c in range(CAP):
                chosen = mine & (mask > 0.5) & (jnp.abs(rank - c) < 0.5)
                picks.append(jnp.where(chosen, 1.0, 0.0).astype(jnp.bfloat16))
        x = x_ref[part, :, :, :head].reshape(BLOCK, head)
        rows = jnp.dot(jnp.concatenate(picks, axis=0), x, preferred_element_type=jnp.float32).astype(jnp.bfloat16)
        for slot in range(4):
            at = pl.multiple_of((group * CAP + slot % CAP) * columns + block * sources, 16)
            picked[slot // CAP, pl.ds(at, sources), :] = rows[slot * sources : (slot + 1) * sources]

    @pl.when(group == pl.num_programs(0) - 1)
    def _():
        units = gate_ref.shape[2]
        for e in range(2):
            out_ref[e, :, :units] = jnp.dot(picked[e], gate_ref[e], preferred_element_type=jnp.float32)
            out_ref[e, :, units:] = jnp.dot(picked[e], up_ref[e], preferred_element_type=jnp.float32)


def head_products(first, x_all, w_gate, w_up):
    columns, groups, tok_count, wide = x_all.shape
    head = wide - LANES
    local_experts, _, units = w_gate.shape
    rows = columns * groups * CAP
    w_spec = pl.BlockSpec((local_experts, head, units), lambda i, first: (0, 0, 0))
    return pl.pallas_call(
        head_kernel,
        out_shape=jax.ShapeDtypeStruct((local_experts, rows, 2 * units), jnp.float32),
        grid_spec=pltpu.PrefetchScalarGridSpec(
            num_scalar_prefetch=1,
            grid=(groups,),
            in_specs=[
                pl.BlockSpec((columns, 1, tok_count, wide), lambda i, first: (0, i, 0, 0)),
                w_spec,
                w_spec,
            ],
            out_specs=pl.BlockSpec((local_experts, rows, 2 * units), lambda i, first: (0, 0, 0)),
            scratch_shapes=[pltpu.VMEM((local_experts, rows, head), jnp.bfloat16)],
        ),
        compiler_params=pltpu.CompilerParams(dimension_semantics=("arbitrary",)),
        cost_estimate=pl.CostEstimate(
            flops=2 * local_experts * rows * 2 * units * head + rows * BLOCK * head,
            bytes_accessed=20 << 20,
            transcendentals=0,
        ),
        name="head_products",
    )(first, x_all, w_gate, w_up)


def hidden_kernel(*refs):
    *slot_refs, down_ref, out_ref = refs

    @pl.when(pl.program_id(0) == 0)
    def _():
        out_ref[...] = jnp.zeros_like(out_ref)

    rows = jnp.concatenate([ref[...] for ref in slot_refs], axis=0)
    out_ref[...] += lax.dot_general(rows, down_ref[0], NT, preferred_element_type=jnp.float32)


def slot_specs(parts, step, skip):
    return [pl.BlockSpec((part.shape[0], step), lambda k: (0, skip + k)) for part in parts]


def hidden_grads(e, parts, w_down):
    _, units, width = w_down.shape
    rows = sum(part.shape[0] for part in parts)
    return pl.pallas_call(
        hidden_kernel,
        out_shape=jax.ShapeDtypeStruct((rows, units), jnp.float32),
        grid=(width // STEP,),
        in_specs=slot_specs(parts, STEP, 0) + [pl.BlockSpec((1, units, STEP), lambda k: (e, 0, k))],
        out_specs=pl.BlockSpec((rows, units), lambda k: (0, 0)),
        compiler_params=pltpu.CompilerParams(dimension_semantics=("arbitrary",)),
        cost_estimate=pl.CostEstimate(flops=2 * rows * units * width, bytes_accessed=5 << 20, transcendentals=0),
        name="hidden_grads",
    )(*parts, w_down)


def late_kernel(*refs):
    *slot_refs, hidden_ref, head_ref, gate_ref, up_ref, out_ref, pre = refs
    step = pl.program_id(0)
    units = gate_ref.shape[2]

    @pl.when(step == 0)
    def _():
        pre[...] = head_ref[0]

    rows = jnp.concatenate([ref[...] for ref in slot_refs], axis=0)
    pre[:, :units] += jnp.dot(rows, gate_ref[0], preferred_element_type=jnp.float32)
    pre[:, units:] += jnp.dot(rows, up_ref[0], preferred_element_type=jnp.float32)

    @pl.when(step == pl.num_programs(0) - 1)
    def _():
        gate_pre, up_pre, grad = pre[:, :units], pre[:, units:], hidden_ref[...]
        s = jax.nn.sigmoid(gate_pre)
        out_ref[:, :units] = (grad * up_pre * s * (1.0 + gate_pre * (1.0 - s))).astype(jnp.bfloat16)
        out_ref[:, units:] = (grad * gate_pre * s).astype(jnp.bfloat16)


def late_grads(e, parts, hidden, head_pre, w_gate, w_up):
    _, width, units = w_gate.shape
    rows = sum(part.shape[0] for part in parts)
    wide = width - HEAD
    w_spec = pl.BlockSpec((1, TAIL_STEP, units), lambda k: (e, HEAD // TAIL_STEP + k, 0))
    return pl.pallas_call(
        late_kernel,
        out_shape=jax.ShapeDtypeStruct((rows, 2 * units), jnp.bfloat16),
        grid=(wide // TAIL_STEP,),
        in_specs=slot_specs(parts, TAIL_STEP, width // TAIL_STEP)
        + [
            pl.BlockSpec((rows, units), lambda k: (0, 0)),
            pl.BlockSpec((1, rows, 2 * units), lambda k: (e, 0, 0)),
            w_spec,
            w_spec,
        ],
        out_specs=pl.BlockSpec((rows, 2 * units), lambda k: (0, 0)),
        scratch_shapes=[pltpu.VMEM((rows, 2 * units), jnp.float32)],
        compiler_params=pltpu.CompilerParams(dimension_semantics=("arbitrary",)),
        cost_estimate=pl.CostEstimate(
            flops=4 * rows * units * wide, bytes_accessed=6 << 20, transcendentals=rows * units
        ),
        name="late_grads",
    )(*parts, hidden, head_pre, w_gate, w_up)


def out_kernel(h0_ref, h1_ref, gate_ref, up_ref, *out_refs):
    units = gate_ref.shape[2]
    for e, h_ref in enumerate((h0_ref, h1_ref)):
        value = lax.dot_general(h_ref[:, :units], gate_ref[e], NT, preferred_element_type=jnp.float32)
        value = value + lax.dot_general(h_ref[:, units:], up_ref[e], NT, preferred_element_type=jnp.float32)
        value = value.astype(jnp.bfloat16)
        part = value.shape[0] // 4
        for r, out_ref in enumerate(out_refs):
            out_ref[e * part : (e + 1) * part, :] = value[r * part : (r + 1) * part]


def out_rows(h, w_gate, w_up, start, stop):
    rows = h[0].shape[0]
    local_experts, width, units = w_gate.shape
    count = local_experts * rows // 4
    h_spec = pl.BlockSpec((rows, 2 * units), lambda n: (0, 0))
    w_spec = pl.BlockSpec((local_experts, OUT_STEP, units), lambda n: (0, start // OUT_STEP + n, 0))
    return pl.pallas_call(
        out_kernel,
        out_shape=[jax.ShapeDtypeStruct((count, stop - start), jnp.bfloat16)] * 4,
        grid=((stop - start) // OUT_STEP,),
        in_specs=[h_spec, h_spec, w_spec, w_spec],
        out_specs=[pl.BlockSpec((count, OUT_STEP), lambda n: (0, n))] * 4,
        compiler_params=pltpu.CompilerParams(dimension_semantics=("arbitrary",)),
        cost_estimate=pl.CostEstimate(
            flops=2 * local_experts * rows * 2 * units * (stop - start), bytes_accessed=8 << 20, transcendentals=0
        ),
        name="out_rows",
    )(*h, w_gate, w_up)


def total(*terms):
    value = terms[0].astype(jnp.float32)
    for term in terms[1:]:
        value = value + term.astype(jnp.float32)
    return value.astype(jnp.bfloat16)


def on_device(tokens, out_grad, route_ids, route_probs, w_gate, w_up, w_down):
    columns = lax.axis_size("expert")
    local_experts = w_gate.shape[0]
    experts = local_experts * columns
    tok_count, width = tokens.shape
    slots = experts * CAP
    per_dest = local_experts * CAP
    first = (lax.axis_index("expert").astype(jnp.int32) * local_experts).reshape(1)

    up_ring = [(i, (i + 1) % 4) for i in range(4)]
    down_ring = [(i, (i + 3) % 4) for i in range(4)]
    far_ring = [(i, (i + 2) % 4) for i in range(4)]

    with jax.named_scope("gather_tokens"):
        ids = jnp.pad(route_ids.astype(jnp.bfloat16), ((0, 0), (0, LANES - route_ids.shape[1])), constant_values=-1)
        mine = jnp.concatenate([tokens[:, :HEAD], ids], axis=1)
        near = jnp.concatenate([mine] + [lax.ppermute(mine, "dp", ring) for ring in (down_ring, far_ring, up_ring)])
        x_all = lax.all_gather(near, "expert", axis=0, tiled=True).reshape(columns, 4, tok_count, HEAD + LANES)

    with jax.named_scope("build_slots"):
        table, slot_scale = slot_table(route_ids, route_probs, experts)
        select = table.astype(jnp.bfloat16)
        tiles = []
        for e in range(2):
            choose = select.reshape(columns, local_experts, CAP, tok_count)[:, e].reshape(columns * CAP, tok_count)
            scale = slot_scale.reshape(columns, local_experts, CAP)[:, e].reshape(columns * CAP, 1)
            g_rows = jnp.dot(choose, out_grad, preferred_element_type=jnp.float32) * scale
            x_rows = jnp.dot(choose, tokens[:, HEAD:], preferred_element_type=jnp.float32)
            rows = jnp.concatenate([g_rows.astype(jnp.bfloat16), x_rows.astype(jnp.bfloat16)], axis=1)
            tiles.append(rows.reshape(columns, CAP, -1))

    def unpack(got):
        got = got.transpose(1, 0, 2)
        return [got[0], got[1]]

    def send(slab):
        return lax.all_to_all(slab, "expert", split_axis=0, concat_axis=0, tiled=True)

    def ring(own):
        right1 = lax.ppermute(own[1], "dp", down_ring)
        left0 = lax.ppermute(own[0], "dp", up_ring)
        right0 = lax.ppermute(own[0], "dp", down_ring)
        left1 = lax.ppermute(own[1], "dp", up_ring)
        return [right0, right1], [left0, left1]

    def ring_on(left0, right1):
        return [lax.ppermute(left0, "dp", up_ring), lax.ppermute(right1, "dp", down_ring)]

    with jax.named_scope("first_expert"):
        own = unpack(send(tiles[0]))
        right, left = ring(own)
        far = ring_on(left[0], right[1])
    with jax.named_scope("second_expert"):
        slab, _ = lax.optimization_barrier((tiles[1], own[0]))
        got, right, left, far = lax.optimization_barrier((send(slab), right, left, far))
        first_parts = own + right + far + left
        hidden0 = hidden_grads(0, first_parts, w_down)
        own = unpack(got)
        right, left = ring(own)
        left[0], right[1], hidden0 = lax.optimization_barrier((left[0], right[1], hidden0))
        far = ring_on(left[0], right[1])
        head_pre = head_products(first, x_all, w_gate, w_up)
        h = [late_grads(0, first_parts, hidden0, head_pre, w_gate, w_up)]
        far, left[1], right[0], h[0] = lax.optimization_barrier((far, left[1], right[0], h[0]))
        second_parts = own + right + far + left

    hidden1 = hidden_grads(1, second_parts, w_down)
    h.append(late_grads(1, second_parts, hidden1, head_pre, w_gate, w_up))

    own_a, right_a, far_a, left_a = out_rows(h, w_gate, w_up, 0, OUT_SPLIT)
    own_b, right_b, far_b, left_b = out_rows(h, w_gate, w_up, OUT_SPLIT, width)
    with jax.named_scope("sum_blocks"):
        from_far = lax.ppermute(far_a, "dp", up_ring)
        from_right_a = lax.ppermute(left_a, "dp", down_ring)
        from_left_a = lax.ppermute(total(right_a, from_far), "dp", up_ring)
        far_b, from_right_a = lax.optimization_barrier((far_b, from_right_a))
        from_far = lax.ppermute(far_b, "dp", down_ring)
        right_b, from_left_a = lax.optimization_barrier((right_b, from_left_a))
        from_left_b = lax.ppermute(right_b, "dp", up_ring)
        left_b = total(left_b, from_far)
        left_b, from_left_a = lax.optimization_barrier((left_b, from_left_a))
        from_right_b = lax.ppermute(left_b, "dp", down_ring)

    results = []
    for terms in ((own_a, from_left_a, from_right_a), (own_b, from_left_b, from_right_b)):
        with jax.named_scope("return_slots"):
            summed = total(*terms)
            cols = summed.shape[1]
            back = summed.reshape(per_dest, columns, cols).transpose(1, 0, 2)
            returned = lax.all_to_all(back, "expert", split_axis=0, concat_axis=0, tiled=True)
        with jax.named_scope("combine"):
            results.append(
                lax.dot_general(
                    select, returned.reshape(slots, cols), (((0,), (0,)), ((), ())),
                    preferred_element_type=jnp.float32,
                ).astype(jnp.bfloat16)
            )
    return jnp.concatenate(results, axis=1)


def solution(mesh):
    placed = (
        P(("dp", "expert"), None),
        P(("dp", "expert"), None),
        P(("dp", "expert"), None),
        P(("dp", "expert"), None),
        P("expert", None, "dp"),
        P("expert", None, "dp"),
        P("expert", "dp", None),
    )
    return jax.shard_map(
        on_device, mesh=mesh, in_specs=placed, out_specs=P(("dp", "expert"), None), check_vma=False
    )
```

```python
import jax
import jax.numpy as jnp
from jax import lax
from jax.experimental import pallas as pl
from jax.experimental.pallas import tpu as pltpu
from jax.sharding import PartitionSpec as P

CAP = 2
LANES = 128
BLOCK = 256
HEAD = 1792
STEP = 1792
TAIL_STEP = 896
OUT_SPLIT = 2304
NT = (((1,), (1,)), ((), ()))


def slot_table(ids, probs, experts):
    tok_count = ids.shape[0]
    named = ids.T[None, :, :] == jnp.arange(experts, dtype=jnp.int32)[:, None, None]
    mask = jnp.any(named, axis=1)
    scale = jnp.sum(jnp.where(named, probs.T[None, :, :], 0.0), axis=1)
    order = jnp.arange(tok_count, dtype=jnp.int32)
    before = (order[:, None] < order[None, :])[None, :, :]
    rank = jnp.sum((mask[:, :, None] & before).astype(jnp.int32), axis=1)
    slots = mask[:, None, :] & (rank[:, None, :] == jnp.arange(CAP, dtype=jnp.int32)[None, :, None])
    slot_scale = jnp.sum(jnp.where(slots, scale[:, None, :], 0.0), axis=2)
    return slots.reshape(experts * CAP, tok_count), slot_scale.reshape(experts * CAP)


def head_kernel(first_ref, x_ref, gate_ref, up_ref, out_ref, picked):
    group = pl.program_id(0)
    head = gate_ref.shape[1]
    columns, _, tok_count, _ = x_ref.shape
    sources = BLOCK // tok_count
    from_tok = lax.broadcasted_iota(jnp.int32, (BLOCK, BLOCK), 0)
    to_tok = lax.broadcasted_iota(jnp.int32, (BLOCK, BLOCK), 1)
    earlier = ((from_tok // tok_count == to_tok // tok_count) & (from_tok < to_tok)).astype(jnp.bfloat16)
    ones = jnp.ones((sources, LANES), jnp.bfloat16)
    mine = lax.broadcasted_iota(jnp.int32, (sources, BLOCK), 0) == (
        lax.broadcasted_iota(jnp.int32, (sources, BLOCK), 1) // tok_count
    )
    for block in range(columns // sources):
        part = pl.ds(block * sources, sources)
        ids = x_ref[part, :, :, head:].reshape(BLOCK, LANES).astype(jnp.float32)
        picks = []
        for e in range(2):
            named = (ids == (first_ref[0] + e).astype(jnp.float32)).astype(jnp.bfloat16)
            mask = lax.dot_general(ones, named, NT, preferred_element_type=jnp.float32)
            rank = jnp.dot(mask.astype(jnp.bfloat16), earlier, preferred_element_type=jnp.float32)
            for c in range(CAP):
                chosen = mine & (mask > 0.5) & (jnp.abs(rank - c) < 0.5)
                picks.append(jnp.where(chosen, 1.0, 0.0).astype(jnp.bfloat16))
        x = x_ref[part, :, :, :head].reshape(BLOCK, head)
        rows = jnp.dot(jnp.concatenate(picks, axis=0), x, preferred_element_type=jnp.float32).astype(jnp.bfloat16)
        for slot in range(4):
            at = pl.multiple_of((group * CAP + slot % CAP) * columns + block * sources, 16)
            picked[slot // CAP, pl.ds(at, sources), :] = rows[slot * sources : (slot + 1) * sources]

    @pl.when(group == pl.num_programs(0) - 1)
    def _():
        units = gate_ref.shape[2]
        for e in range(2):
            out_ref[e, :, :units] = jnp.dot(picked[e], gate_ref[e], preferred_element_type=jnp.float32)
            out_ref[e, :, units:] = jnp.dot(picked[e], up_ref[e], preferred_element_type=jnp.float32)


def head_products(first, x_all, w_gate, w_up):
    columns, groups, tok_count, wide = x_all.shape
    head = wide - LANES
    local_experts, _, units = w_gate.shape
    rows = columns * groups * CAP
    w_spec = pl.BlockSpec((local_experts, head, units), lambda i, first: (0, 0, 0))
    return pl.pallas_call(
        head_kernel,
        out_shape=jax.ShapeDtypeStruct((local_experts, rows, 2 * units), jnp.float32),
        grid_spec=pltpu.PrefetchScalarGridSpec(
            num_scalar_prefetch=1,
            grid=(groups,),
            in_specs=[
                pl.BlockSpec((columns, 1, tok_count, wide), lambda i, first: (0, i, 0, 0)),
                w_spec,
                w_spec,
            ],
            out_specs=pl.BlockSpec((local_experts, rows, 2 * units), lambda i, first: (0, 0, 0)),
            scratch_shapes=[pltpu.VMEM((local_experts, rows, head), jnp.bfloat16)],
        ),
        compiler_params=pltpu.CompilerParams(dimension_semantics=("arbitrary",)),
        cost_estimate=pl.CostEstimate(
            flops=2 * local_experts * rows * 2 * units * head + rows * BLOCK * head,
            bytes_accessed=20 << 20,
            transcendentals=0,
        ),
        name="head_products",
    )(first, x_all, w_gate, w_up)


def hidden_kernel(*refs):
    *slot_refs, down_ref, out_ref = refs

    @pl.when(pl.program_id(0) == 0)
    def _():
        out_ref[...] = jnp.zeros_like(out_ref)

    rows = jnp.concatenate([ref[...] for ref in slot_refs], axis=0)
    out_ref[...] += lax.dot_general(rows, down_ref[0], NT, preferred_element_type=jnp.float32)


def slot_specs(parts, step, skip):
    return [pl.BlockSpec((part.shape[0], step), lambda k: (0, skip + k)) for part in parts]


def hidden_grads(e, parts, w_down):
    _, units, width = w_down.shape
    rows = sum(part.shape[0] for part in parts)
    return pl.pallas_call(
        hidden_kernel,
        out_shape=jax.ShapeDtypeStruct((rows, units), jnp.float32),
        grid=(width // STEP,),
        in_specs=slot_specs(parts, STEP, 0) + [pl.BlockSpec((1, units, STEP), lambda k: (e, 0, k))],
        out_specs=pl.BlockSpec((rows, units), lambda k: (0, 0)),
        compiler_params=pltpu.CompilerParams(dimension_semantics=("arbitrary",)),
        cost_estimate=pl.CostEstimate(flops=2 * rows * units * width, bytes_accessed=5 << 20, transcendentals=0),
        name="hidden_grads",
    )(*parts, w_down)


def late_kernel(*refs):
    *slot_refs, hidden_ref, head_ref, gate_ref, up_ref, out_ref, pre = refs
    step = pl.program_id(0)
    units = gate_ref.shape[2]

    @pl.when(step == 0)
    def _():
        pre[...] = head_ref[0]

    rows = jnp.concatenate([ref[...] for ref in slot_refs], axis=0)
    pre[:, :units] += jnp.dot(rows, gate_ref[0], preferred_element_type=jnp.float32)
    pre[:, units:] += jnp.dot(rows, up_ref[0], preferred_element_type=jnp.float32)

    @pl.when(step == pl.num_programs(0) - 1)
    def _():
        gate_pre, up_pre, grad = pre[:, :units], pre[:, units:], hidden_ref[...]
        s = jax.nn.sigmoid(gate_pre)
        out_ref[:, :units] = (grad * up_pre * s * (1.0 + gate_pre * (1.0 - s))).astype(jnp.bfloat16)
        out_ref[:, units:] = (grad * gate_pre * s).astype(jnp.bfloat16)


def late_grads(e, parts, hidden, head_pre, w_gate, w_up):
    _, width, units = w_gate.shape
    rows = sum(part.shape[0] for part in parts)
    wide = width - HEAD
    w_spec = pl.BlockSpec((1, TAIL_STEP, units), lambda k: (e, HEAD // TAIL_STEP + k, 0))
    return pl.pallas_call(
        late_kernel,
        out_shape=jax.ShapeDtypeStruct((rows, 2 * units), jnp.bfloat16),
        grid=(wide // TAIL_STEP,),
        in_specs=slot_specs(parts, TAIL_STEP, width // TAIL_STEP)
        + [
            pl.BlockSpec((rows, units), lambda k: (0, 0)),
            pl.BlockSpec((1, rows, 2 * units), lambda k: (e, 0, 0)),
            w_spec,
            w_spec,
        ],
        out_specs=pl.BlockSpec((rows, 2 * units), lambda k: (0, 0)),
        scratch_shapes=[pltpu.VMEM((rows, 2 * units), jnp.float32)],
        compiler_params=pltpu.CompilerParams(dimension_semantics=("arbitrary",)),
        cost_estimate=pl.CostEstimate(
            flops=4 * rows * units * wide, bytes_accessed=6 << 20, transcendentals=rows * units
        ),
        name="late_grads",
    )(*parts, hidden, head_pre, w_gate, w_up)


def out_kernel(h0_ref, h1_ref, gate_ref, up_ref, *out_refs):
    units = gate_ref.shape[2]
    for e, h_ref in enumerate((h0_ref, h1_ref)):
        value = lax.dot_general(h_ref[:, :units], gate_ref[e], NT, preferred_element_type=jnp.float32)
        value = value + lax.dot_general(h_ref[:, units:], up_ref[e], NT, preferred_element_type=jnp.float32)
        value = value.astype(jnp.bfloat16)
        part = value.shape[0] // 4
        for r, out_ref in enumerate(out_refs):
            out_ref[e * part : (e + 1) * part, :] = value[r * part : (r + 1) * part]


def out_rows(h, w_gate, w_up, start, stop, step):
    rows = h[0].shape[0]
    local_experts, width, units = w_gate.shape
    count = local_experts * rows // 4
    h_spec = pl.BlockSpec((rows, 2 * units), lambda n: (0, 0))
    w_spec = pl.BlockSpec((local_experts, step, units), lambda n: (0, start // step + n, 0))
    return pl.pallas_call(
        out_kernel,
        out_shape=[jax.ShapeDtypeStruct((count, stop - start), jnp.bfloat16)] * 4,
        grid=((stop - start) // step,),
        in_specs=[h_spec, h_spec, w_spec, w_spec],
        out_specs=[pl.BlockSpec((count, step), lambda n: (0, n))] * 4,
        compiler_params=pltpu.CompilerParams(dimension_semantics=("arbitrary",)),
        cost_estimate=pl.CostEstimate(
            flops=2 * local_experts * rows * 2 * units * (stop - start), bytes_accessed=8 << 20, transcendentals=0
        ),
        name="out_rows",
    )(*h, w_gate, w_up)


def total(*terms):
    value = terms[0].astype(jnp.float32)
    for term in terms[1:]:
        value = value + term.astype(jnp.float32)
    return value.astype(jnp.bfloat16)


def on_device(tokens, out_grad, route_ids, route_probs, w_gate, w_up, w_down):
    columns = lax.axis_size("expert")
    local_experts = w_gate.shape[0]
    experts = local_experts * columns
    tok_count, width = tokens.shape
    slots = experts * CAP
    per_dest = local_experts * CAP
    first = (lax.axis_index("expert").astype(jnp.int32) * local_experts).reshape(1)

    up_ring = [(i, (i + 1) % 4) for i in range(4)]
    down_ring = [(i, (i + 3) % 4) for i in range(4)]
    far_ring = [(i, (i + 2) % 4) for i in range(4)]

    with jax.named_scope("gather_tokens"):
        ids = jnp.pad(route_ids.astype(jnp.bfloat16), ((0, 0), (0, LANES - route_ids.shape[1])), constant_values=-1)
        mine = jnp.concatenate([tokens[:, :HEAD], ids], axis=1)
        pieces = [mine] + [lax.ppermute(mine, "dp", ring) for ring in (down_ring, far_ring, up_ring)]

    with jax.named_scope("build_slots"):
        table, slot_scale = slot_table(route_ids, route_probs, experts)
        select = table.astype(jnp.bfloat16)
        tiles = []
        for e in range(2):
            choose = select.reshape(columns, local_experts, CAP, tok_count)[:, e].reshape(columns * CAP, tok_count)
            scale = slot_scale.reshape(columns, local_experts, CAP)[:, e].reshape(columns * CAP, 1)
            g_rows = jnp.dot(choose, out_grad, preferred_element_type=jnp.float32) * scale
            x_rows = jnp.dot(choose, tokens[:, HEAD:], preferred_element_type=jnp.float32)
            rows = jnp.concatenate([g_rows.astype(jnp.bfloat16), x_rows.astype(jnp.bfloat16)], axis=1)
            tiles.append(rows.reshape(columns, CAP, -1))

    with jax.named_scope("gather_tokens"):
        tiles[0], pieces = lax.optimization_barrier((tiles[0], pieces))
        near = jnp.concatenate(pieces)
        x_all = lax.all_gather(near, "expert", axis=0, tiled=True).reshape(columns, 4, tok_count, HEAD + LANES)

    def unpack(got):
        got = got.transpose(1, 0, 2)
        return [got[0], got[1]]

    def send(slab):
        return lax.all_to_all(slab, "expert", split_axis=0, concat_axis=0, tiled=True)

    def ring(own):
        right1 = lax.ppermute(own[1], "dp", down_ring)
        left0 = lax.ppermute(own[0], "dp", up_ring)
        right0 = lax.ppermute(own[0], "dp", down_ring)
        left1 = lax.ppermute(own[1], "dp", up_ring)
        return [right0, right1], [left0, left1]

    def ring_on(left0, right1):
        return [lax.ppermute(left0, "dp", up_ring), lax.ppermute(right1, "dp", down_ring)]

    with jax.named_scope("first_expert"):
        own = unpack(send(tiles[0]))
        right, left = ring(own)
        far = ring_on(left[0], right[1])
    with jax.named_scope("second_expert"):
        slab, _ = lax.optimization_barrier((tiles[1], own[0]))
        got, right, left, far = lax.optimization_barrier((send(slab), right, left, far))
        first_parts = own + right + far + left
        hidden0 = hidden_grads(0, first_parts, w_down)
        own = unpack(got)
        right, left = ring(own)
        left[0], right[1], hidden0 = lax.optimization_barrier((left[0], right[1], hidden0))
        far = ring_on(left[0], right[1])
        head_pre = head_products(first, x_all, w_gate, w_up)
        h = [late_grads(0, first_parts, hidden0, head_pre, w_gate, w_up)]
        far, left[1], right[0], h[0] = lax.optimization_barrier((far, left[1], right[0], h[0]))
        second_parts = own + right + far + left

    hidden1 = hidden_grads(1, second_parts, w_down)
    h.append(late_grads(1, second_parts, hidden1, head_pre, w_gate, w_up))

    own_a, right_a, far_a, left_a = out_rows(h, w_gate, w_up, OUT_SPLIT, width, 256)
    own_b, right_b, far_b, left_b = out_rows(h, w_gate, w_up, 0, OUT_SPLIT, 768)
    with jax.named_scope("sum_blocks"):
        from_far = lax.ppermute(far_a, "dp", up_ring)
        from_right_a = lax.ppermute(left_a, "dp", down_ring)
        from_left_a = lax.ppermute(total(right_a, from_far), "dp", up_ring)
        far_b, from_right_a = lax.optimization_barrier((far_b, from_right_a))
        from_far = lax.ppermute(far_b, "dp", down_ring)
        right_b, from_left_a = lax.optimization_barrier((right_b, from_left_a))
        from_left_b = lax.ppermute(right_b, "dp", up_ring)
        left_b = total(left_b, from_far)
        left_b, from_left_a = lax.optimization_barrier((left_b, from_left_a))
        from_right_b = lax.ppermute(left_b, "dp", down_ring)

    results = []
    for terms in ((own_a, from_left_a, from_right_a), (own_b, from_left_b, from_right_b)):
        with jax.named_scope("return_slots"):
            summed = total(*terms)
            cols = summed.shape[1]
            back = summed.reshape(per_dest, columns, cols).transpose(1, 0, 2)
            returned = lax.all_to_all(back, "expert", split_axis=0, concat_axis=0, tiled=True)
        with jax.named_scope("combine"):
            results.append(
                lax.dot_general(
                    select, returned.reshape(slots, cols), (((0,), (0,)), ((), ())),
                    preferred_element_type=jnp.float32,
                ).astype(jnp.bfloat16)
            )
    return jnp.concatenate(results[::-1], axis=1)


def solution(mesh):
    placed = (
        P(("dp", "expert"), None),
        P(("dp", "expert"), None),
        P(("dp", "expert"), None),
        P(("dp", "expert"), None),
        P("expert", None, "dp"),
        P("expert", None, "dp"),
        P("expert", "dp", None),
    )
    return jax.shard_map(
        on_device, mesh=mesh, in_specs=placed, out_specs=P(("dp", "expert"), None), check_vma=False
    )
```

```python
import jax
import jax.numpy as jnp
from jax import lax
from jax.experimental import pallas as pl
from jax.experimental.pallas import tpu as pltpu
from jax.sharding import PartitionSpec as P

CAP = 2
LANES = 128
BLOCK = 256
HEAD = 2048
STEP = 1792
TAIL_STEP = 512
OUT_SPLIT = 1280
NT = (((1,), (1,)), ((), ()))


def slot_table(ids, probs, experts):
    tok_count = ids.shape[0]
    named = ids.T[None, :, :] == jnp.arange(experts, dtype=jnp.int32)[:, None, None]
    mask = jnp.any(named, axis=1)
    scale = jnp.sum(jnp.where(named, probs.T[None, :, :], 0.0), axis=1)
    order = jnp.arange(tok_count, dtype=jnp.int32)
    before = (order[:, None] < order[None, :])[None, :, :]
    rank = jnp.sum((mask[:, :, None] & before).astype(jnp.int32), axis=1)
    slots = mask[:, None, :] & (rank[:, None, :] == jnp.arange(CAP, dtype=jnp.int32)[None, :, None])
    slot_scale = jnp.sum(jnp.where(slots, scale[:, None, :], 0.0), axis=2)
    return slots.reshape(experts * CAP, tok_count), slot_scale.reshape(experts * CAP)


def unit_grads(pre, grad, out_ref):
    units = grad.shape[1]
    gate_pre, up_pre = pre[:, :units], pre[:, units:]
    s = jax.nn.sigmoid(gate_pre)
    out_ref[:, :units] = (grad * up_pre * s * (1.0 + gate_pre * (1.0 - s))).astype(jnp.bfloat16)
    out_ref[:, units:] = (grad * gate_pre * s).astype(jnp.bfloat16)


def head_kernel(first_ref, x_ref, gate_ref, up_ref, tail_ref, hidden_ref, out_ref, pre_ref, picked):
    group = pl.program_id(0)
    head = gate_ref.shape[1]
    columns, _, tok_count, _ = x_ref.shape
    sources = BLOCK // tok_count
    from_tok = lax.broadcasted_iota(jnp.int32, (BLOCK, BLOCK), 0)
    to_tok = lax.broadcasted_iota(jnp.int32, (BLOCK, BLOCK), 1)
    earlier = ((from_tok // tok_count == to_tok // tok_count) & (from_tok < to_tok)).astype(jnp.bfloat16)
    ones = jnp.ones((sources, LANES), jnp.bfloat16)
    mine = lax.broadcasted_iota(jnp.int32, (sources, BLOCK), 0) == (
        lax.broadcasted_iota(jnp.int32, (sources, BLOCK), 1) // tok_count
    )
    for block in range(columns // sources):
        part = pl.ds(block * sources, sources)
        ids = x_ref[part, :, :, head:].reshape(BLOCK, LANES).astype(jnp.float32)
        picks = []
        for e in range(2):
            named = (ids == (first_ref[0] + e).astype(jnp.float32)).astype(jnp.bfloat16)
            mask = lax.dot_general(ones, named, NT, preferred_element_type=jnp.float32)
            rank = jnp.dot(mask.astype(jnp.bfloat16), earlier, preferred_element_type=jnp.float32)
            for c in range(CAP):
                chosen = mine & (mask > 0.5) & (jnp.abs(rank - c) < 0.5)
                picks.append(jnp.where(chosen, 1.0, 0.0).astype(jnp.bfloat16))
        x = x_ref[part, :, :, :head].reshape(BLOCK, head)
        rows = jnp.dot(jnp.concatenate(picks, axis=0), x, preferred_element_type=jnp.float32).astype(jnp.bfloat16)
        for slot in range(4):
            at = pl.multiple_of((group * CAP + slot % CAP) * columns + block * sources, 16)
            picked[slot // CAP, pl.ds(at, sources), :] = rows[slot * sources : (slot + 1) * sources]

    @pl.when(group == pl.num_programs(0) - 1)
    def _():
        units = gate_ref.shape[2]
        for e in range(2):
            gate_pre = jnp.dot(picked[e], gate_ref[e], preferred_element_type=jnp.float32)
            up_pre = jnp.dot(picked[e], up_ref[e], preferred_element_type=jnp.float32)
            if e == 0:
                pre = tail_ref[...] + jnp.concatenate([gate_pre, up_pre], axis=1)
                unit_grads(pre, hidden_ref[...], out_ref)
            else:
                pre_ref[:, :units] = gate_pre
                pre_ref[:, units:] = up_pre


def head_products(first, x_all, w_gate, w_up, tail, hidden):
    columns, groups, tok_count, wide = x_all.shape
    head = wide - LANES
    local_experts, _, units = w_gate.shape
    rows = columns * groups * CAP
    w_spec = pl.BlockSpec((local_experts, head, units), lambda i, first: (0, 0, 0))
    return pl.pallas_call(
        head_kernel,
        out_shape=[
            jax.ShapeDtypeStruct((rows, 2 * units), jnp.bfloat16),
            jax.ShapeDtypeStruct((rows, 2 * units), jnp.float32),
        ],
        grid_spec=pltpu.PrefetchScalarGridSpec(
            num_scalar_prefetch=1,
            grid=(groups,),
            in_specs=[
                pl.BlockSpec((columns, 1, tok_count, wide), lambda i, first: (0, i, 0, 0)),
                w_spec,
                w_spec,
                pl.BlockSpec((rows, 2 * units), lambda i, first: (0, 0)),
                pl.BlockSpec((rows, units), lambda i, first: (0, 0)),
            ],
            out_specs=[pl.BlockSpec((rows, 2 * units), lambda i, first: (0, 0))] * 2,
            scratch_shapes=[pltpu.VMEM((local_experts, rows, head), jnp.bfloat16)],
        ),
        compiler_params=pltpu.CompilerParams(dimension_semantics=("arbitrary",)),
        cost_estimate=pl.CostEstimate(
            flops=2 * local_experts * rows * 2 * units * head + rows * BLOCK * head,
            bytes_accessed=20 << 20,
            transcendentals=0,
        ),
        name="head_products",
    )(first, x_all, w_gate, w_up, tail, hidden)


def hidden_kernel(*refs):
    *slot_refs, down_ref, out_ref = refs

    @pl.when(pl.program_id(0) == 0)
    def _():
        out_ref[...] = jnp.zeros_like(out_ref)

    rows = jnp.concatenate([ref[...] for ref in slot_refs], axis=0)
    out_ref[...] += lax.dot_general(rows, down_ref[0], NT, preferred_element_type=jnp.float32)


def slot_specs(parts, step, skip):
    return [pl.BlockSpec((part.shape[0], step), lambda k: (0, skip + k)) for part in parts]


def hidden_grads(e, parts, w_down):
    _, units, width = w_down.shape
    rows = sum(part.shape[0] for part in parts)
    return pl.pallas_call(
        hidden_kernel,
        out_shape=jax.ShapeDtypeStruct((rows, units), jnp.float32),
        grid=(width // STEP,),
        in_specs=slot_specs(parts, STEP, 0) + [pl.BlockSpec((1, units, STEP), lambda k: (e, 0, k))],
        out_specs=pl.BlockSpec((rows, units), lambda k: (0, 0)),
        compiler_params=pltpu.CompilerParams(dimension_semantics=("arbitrary",)),
        cost_estimate=pl.CostEstimate(flops=2 * rows * units * width, bytes_accessed=5 << 20, transcendentals=0),
        name="hidden_grads",
    )(*parts, w_down)


def tail_kernel(*refs):
    *slot_refs, gate_ref, up_ref, pre = refs
    units = gate_ref.shape[2]

    @pl.when(pl.program_id(0) == 0)
    def _():
        pre[...] = jnp.zeros_like(pre)

    rows = jnp.concatenate([ref[...] for ref in slot_refs], axis=0)
    pre[:, :units] += jnp.dot(rows, gate_ref[0], preferred_element_type=jnp.float32)
    pre[:, units:] += jnp.dot(rows, up_ref[0], preferred_element_type=jnp.float32)


def late_kernel(*refs):
    *slot_refs, hidden_ref, head_ref, gate_ref, up_ref, out_ref, pre = refs
    step = pl.program_id(0)
    units = gate_ref.shape[2]

    @pl.when(step == 0)
    def _():
        pre[...] = head_ref[...]

    rows = jnp.concatenate([ref[...] for ref in slot_refs], axis=0)
    pre[:, :units] += jnp.dot(rows, gate_ref[0], preferred_element_type=jnp.float32)
    pre[:, units:] += jnp.dot(rows, up_ref[0], preferred_element_type=jnp.float32)

    @pl.when(step == pl.num_programs(0) - 1)
    def _():
        unit_grads(pre[...], hidden_ref[...], out_ref)


def late_specs(e, parts, w_gate):
    _, width, units = w_gate.shape
    w_spec = pl.BlockSpec((1, TAIL_STEP, units), lambda k: (e, HEAD // TAIL_STEP + k, 0))
    rows = sum(part.shape[0] for part in parts)
    whole = pl.BlockSpec((rows, 2 * units), lambda k: (0, 0))
    cost = pl.CostEstimate(
        flops=4 * rows * units * (width - HEAD), bytes_accessed=6 << 20, transcendentals=rows * units
    )
    return slot_specs(parts, TAIL_STEP, width // TAIL_STEP), [w_spec, w_spec], whole, cost


def tail_products(e, parts, w_gate, w_up):
    slots, weights, whole, cost = late_specs(e, parts, w_gate)
    return pl.pallas_call(
        tail_kernel,
        out_shape=jax.ShapeDtypeStruct(whole.block_shape, jnp.float32),
        grid=((w_gate.shape[1] - HEAD) // TAIL_STEP,),
        in_specs=slots + weights,
        out_specs=whole,
        compiler_params=pltpu.CompilerParams(dimension_semantics=("arbitrary",)),
        cost_estimate=cost,
        name="tail_products",
    )(*parts, w_gate, w_up)


def late_grads(e, parts, hidden, head_pre, w_gate, w_up):
    slots, weights, whole, cost = late_specs(e, parts, w_gate)
    return pl.pallas_call(
        late_kernel,
        out_shape=jax.ShapeDtypeStruct(whole.block_shape, jnp.bfloat16),
        grid=((w_gate.shape[1] - HEAD) // TAIL_STEP,),
        in_specs=slots + [pl.BlockSpec(hidden.shape, lambda k: (0, 0)), whole] + weights,
        out_specs=whole,
        scratch_shapes=[pltpu.VMEM(whole.block_shape, jnp.float32)],
        compiler_params=pltpu.CompilerParams(dimension_semantics=("arbitrary",)),
        cost_estimate=cost,
        name="late_grads",
    )(*parts, hidden, head_pre, w_gate, w_up)


def out_kernel(h0_ref, h1_ref, gate_ref, up_ref, *out_refs):
    units = gate_ref.shape[2]
    for e, h_ref in enumerate((h0_ref, h1_ref)):
        value = lax.dot_general(h_ref[:, :units], gate_ref[e], NT, preferred_element_type=jnp.float32)
        value = value + lax.dot_general(h_ref[:, units:], up_ref[e], NT, preferred_element_type=jnp.float32)
        value = value.astype(jnp.bfloat16)
        part = value.shape[0] // 4
        for r, out_ref in enumerate(out_refs):
            out_ref[e * part : (e + 1) * part, :] = value[r * part : (r + 1) * part]


def out_rows(h, w_gate, w_up, start, stop, step):
    rows = h[0].shape[0]
    local_experts, width, units = w_gate.shape
    count = local_experts * rows // 4
    h_spec = pl.BlockSpec((rows, 2 * units), lambda n: (0, 0))
    w_spec = pl.BlockSpec((local_experts, step, units), lambda n: (0, start // step + n, 0))
    return pl.pallas_call(
        out_kernel,
        out_shape=[jax.ShapeDtypeStruct((count, stop - start), jnp.bfloat16)] * 4,
        grid=((stop - start) // step,),
        in_specs=[h_spec, h_spec, w_spec, w_spec],
        out_specs=[pl.BlockSpec((count, step), lambda n: (0, n))] * 4,
        compiler_params=pltpu.CompilerParams(dimension_semantics=("arbitrary",)),
        cost_estimate=pl.CostEstimate(
            flops=2 * local_experts * rows * 2 * units * (stop - start), bytes_accessed=8 << 20, transcendentals=0
        ),
        name="out_rows",
    )(*h, w_gate, w_up)


def total(*terms):
    value = terms[0].astype(jnp.float32)
    for term in terms[1:]:
        value = value + term.astype(jnp.float32)
    return value.astype(jnp.bfloat16)


def on_device(tokens, out_grad, route_ids, route_probs, w_gate, w_up, w_down):
    columns = lax.axis_size("expert")
    local_experts = w_gate.shape[0]
    experts = local_experts * columns
    tok_count, width = tokens.shape
    slots = experts * CAP
    per_dest = local_experts * CAP
    first = (lax.axis_index("expert").astype(jnp.int32) * local_experts).reshape(1)

    up_ring = [(i, (i + 1) % 4) for i in range(4)]
    down_ring = [(i, (i + 3) % 4) for i in range(4)]
    far_ring = [(i, (i + 2) % 4) for i in range(4)]

    with jax.named_scope("gather_tokens"):
        ids = jnp.pad(route_ids.astype(jnp.bfloat16), ((0, 0), (0, LANES - route_ids.shape[1])), constant_values=-1)
        mine = jnp.concatenate([tokens[:, :HEAD], ids], axis=1)
        pieces = [mine] + [lax.ppermute(mine, "dp", ring) for ring in (down_ring, far_ring, up_ring)]

    with jax.named_scope("build_slots"):
        table, slot_scale = slot_table(route_ids, route_probs, experts)
        select = table.astype(jnp.bfloat16)
        tiles = []
        for e in range(2):
            choose = select.reshape(columns, local_experts, CAP, tok_count)[:, e].reshape(columns * CAP, tok_count)
            scale = slot_scale.reshape(columns, local_experts, CAP)[:, e].reshape(columns * CAP, 1)
            g_rows = jnp.dot(choose, out_grad, preferred_element_type=jnp.float32) * scale
            x_rows = jnp.dot(choose, tokens[:, HEAD:], preferred_element_type=jnp.float32)
            rows = jnp.concatenate([g_rows.astype(jnp.bfloat16), x_rows.astype(jnp.bfloat16)], axis=1)
            tiles.append(rows.reshape(columns, CAP, -1))

    with jax.named_scope("gather_tokens"):
        tiles[0], pieces = lax.optimization_barrier((tiles[0], pieces))
        near = jnp.concatenate(pieces)
        x_all = lax.all_gather(near, "expert", axis=0, tiled=True).reshape(columns, 4, tok_count, HEAD + LANES)

    def unpack(got):
        got = got.transpose(1, 0, 2)
        return [got[0], got[1]]

    def send(slab):
        return lax.all_to_all(slab, "expert", split_axis=0, concat_axis=0, tiled=True)

    def ring(own):
        right1 = lax.ppermute(own[1], "dp", down_ring)
        left0 = lax.ppermute(own[0], "dp", up_ring)
        right0 = lax.ppermute(own[0], "dp", down_ring)
        left1 = lax.ppermute(own[1], "dp", up_ring)
        return [right0, right1], [left0, left1]

    def ring_on(left0, right1):
        return [lax.ppermute(left0, "dp", up_ring), lax.ppermute(right1, "dp", down_ring)]

    with jax.named_scope("first_expert"):
        own = unpack(send(tiles[0]))
        right, left = ring(own)
        far = ring_on(left[0], right[1])
    with jax.named_scope("second_expert"):
        slab, _ = lax.optimization_barrier((tiles[1], own[0]))
        got, right, left, far = lax.optimization_barrier((send(slab), right, left, far))
        first_parts = own + right + far + left
        hidden0 = hidden_grads(0, first_parts, w_down)
        tail0 = tail_products(0, first_parts, w_gate, w_up)
        own = unpack(got)
        right, left = ring(own)
        left[0], right[1], hidden0, tail0 = lax.optimization_barrier((left[0], right[1], hidden0, tail0))
        far = ring_on(left[0], right[1])
        h0, head_pre = head_products(first, x_all, w_gate, w_up, tail0, hidden0)
        far, left[1], right[0], h0 = lax.optimization_barrier((far, left[1], right[0], h0))
        second_parts = own + right + far + left

    hidden1 = hidden_grads(1, second_parts, w_down)
    h = [h0, late_grads(1, second_parts, hidden1, head_pre, w_gate, w_up)]

    own_a, right_a, far_a, left_a = out_rows(h, w_gate, w_up, 0, OUT_SPLIT, 640)
    own_b, right_b, far_b, left_b = out_rows(h, w_gate, w_up, OUT_SPLIT, width, 256)
    with jax.named_scope("sum_blocks"):
        from_far = lax.ppermute(far_a, "dp", up_ring)
        from_right_a = lax.ppermute(left_a, "dp", down_ring)
        from_left_a = lax.ppermute(total(right_a, from_far), "dp", up_ring)
        far_b, from_right_a = lax.optimization_barrier((far_b, from_right_a))
        from_far = lax.ppermute(far_b, "dp", down_ring)
        right_b, from_left_a = lax.optimization_barrier((right_b, from_left_a))
        from_left_b = lax.ppermute(right_b, "dp", up_ring)
        left_b = total(left_b, from_far)
        left_b, from_left_a = lax.optimization_barrier((left_b, from_left_a))
        from_right_b = lax.ppermute(left_b, "dp", down_ring)

    results = []
    for terms in ((own_a, from_left_a, from_right_a), (own_b, from_left_b, from_right_b)):
        with jax.named_scope("return_slots"):
            summed = total(*terms)
            cols = summed.shape[1]
            back = summed.reshape(per_dest, columns, cols).transpose(1, 0, 2)
            returned = lax.all_to_all(back, "expert", split_axis=0, concat_axis=0, tiled=True)
        with jax.named_scope("combine"):
            results.append(
                lax.dot_general(
                    select, returned.reshape(slots, cols), (((0,), (0,)), ((), ())),
                    preferred_element_type=jnp.float32,
                ).astype(jnp.bfloat16)
            )
    return jnp.concatenate(results, axis=1)


def solution(mesh):
    placed = (
        P(("dp", "expert"), None),
        P(("dp", "expert"), None),
        P(("dp", "expert"), None),
        P(("dp", "expert"), None),
        P("expert", None, "dp"),
        P("expert", None, "dp"),
        P("expert", "dp", None),
    )
    return jax.shard_map(
        on_device, mesh=mesh, in_specs=placed, out_specs=P(("dp", "expert"), None), check_vma=False
    )
```

```python
import jax
import jax.numpy as jnp
from jax import lax
from jax.experimental import pallas as pl
from jax.experimental.pallas import tpu as pltpu
from jax.sharding import PartitionSpec as P

CAP = 2
LANES = 128
BLOCK = 256
HEAD = 2048
STEP = 1792
TAIL_STEP = 512
OUT_SPLIT = 1280
NT = (((1,), (1,)), ((), ()))


def slot_table(ids, probs, experts):
    tok_count = ids.shape[0]
    named = ids.T[None, :, :] == jnp.arange(experts, dtype=jnp.int32)[:, None, None]
    mask = jnp.any(named, axis=1)
    scale = jnp.sum(jnp.where(named, probs.T[None, :, :], 0.0), axis=1)
    order = jnp.arange(tok_count, dtype=jnp.int32)
    before = (order[:, None] < order[None, :])[None, :, :]
    rank = jnp.sum((mask[:, :, None] & before).astype(jnp.int32), axis=1)
    slots = mask[:, None, :] & (rank[:, None, :] == jnp.arange(CAP, dtype=jnp.int32)[None, :, None])
    slot_scale = jnp.sum(jnp.where(slots, scale[:, None, :], 0.0), axis=2)
    return slots.reshape(experts * CAP, tok_count), slot_scale.reshape(experts * CAP)


def unit_grads(pre, grad, out_ref):
    units = grad.shape[1]
    gate_pre, up_pre = pre[:, :units], pre[:, units:]
    s = jax.nn.sigmoid(gate_pre)
    out_ref[:, :units] = (grad * up_pre * s * (1.0 + gate_pre * (1.0 - s))).astype(jnp.bfloat16)
    out_ref[:, units:] = (grad * gate_pre * s).astype(jnp.bfloat16)


def head_kernel(first_ref, x_ref, gate_ref, up_ref, tail_ref, hidden_ref, out_ref, pre_ref, picked):
    group = pl.program_id(0)
    head = gate_ref.shape[1]
    columns, _, tok_count, _ = x_ref.shape
    sources = BLOCK // tok_count
    from_tok = lax.broadcasted_iota(jnp.int32, (BLOCK, BLOCK), 0)
    to_tok = lax.broadcasted_iota(jnp.int32, (BLOCK, BLOCK), 1)
    earlier = ((from_tok // tok_count == to_tok // tok_count) & (from_tok < to_tok)).astype(jnp.bfloat16)
    ones = jnp.ones((sources, LANES), jnp.bfloat16)
    mine = lax.broadcasted_iota(jnp.int32, (sources, BLOCK), 0) == (
        lax.broadcasted_iota(jnp.int32, (sources, BLOCK), 1) // tok_count
    )
    for block in range(columns // sources):
        part = pl.ds(block * sources, sources)
        ids = x_ref[part, :, :, head:].reshape(BLOCK, LANES).astype(jnp.float32)
        picks = []
        for e in range(2):
            named = (ids == (first_ref[0] + e).astype(jnp.float32)).astype(jnp.bfloat16)
            mask = lax.dot_general(ones, named, NT, preferred_element_type=jnp.float32)
            rank = jnp.dot(mask.astype(jnp.bfloat16), earlier, preferred_element_type=jnp.float32)
            for c in range(CAP):
                chosen = mine & (mask > 0.5) & (jnp.abs(rank - c) < 0.5)
                picks.append(jnp.where(chosen, 1.0, 0.0).astype(jnp.bfloat16))
        x = x_ref[part, :, :, :head].reshape(BLOCK, head)
        rows = jnp.dot(jnp.concatenate(picks, axis=0), x, preferred_element_type=jnp.float32).astype(jnp.bfloat16)
        for slot in range(4):
            at = pl.multiple_of((group * CAP + slot % CAP) * columns + block * sources, 16)
            picked[slot // CAP, pl.ds(at, sources), :] = rows[slot * sources : (slot + 1) * sources]

    @pl.when(group == pl.num_programs(0) - 1)
    def _():
        units = gate_ref.shape[2]
        for e in range(2):
            gate_pre = jnp.dot(picked[e], gate_ref[e], preferred_element_type=jnp.float32)
            up_pre = jnp.dot(picked[e], up_ref[e], preferred_element_type=jnp.float32)
            if e == 0:
                pre = tail_ref[...] + jnp.concatenate([gate_pre, up_pre], axis=1)
                unit_grads(pre, hidden_ref[...], out_ref)
            else:
                pre_ref[:, :units] = gate_pre
                pre_ref[:, units:] = up_pre


def head_products(first, x_all, w_gate, w_up, tail, hidden):
    columns, groups, tok_count, wide = x_all.shape
    head = wide - LANES
    local_experts, _, units = w_gate.shape
    rows = columns * groups * CAP
    w_spec = pl.BlockSpec((local_experts, head, units), lambda i, first: (0, 0, 0))
    return pl.pallas_call(
        head_kernel,
        out_shape=[
            jax.ShapeDtypeStruct((rows, 2 * units), jnp.bfloat16),
            jax.ShapeDtypeStruct((rows, 2 * units), jnp.float32),
        ],
        grid_spec=pltpu.PrefetchScalarGridSpec(
            num_scalar_prefetch=1,
            grid=(groups,),
            in_specs=[
                pl.BlockSpec((columns, 1, tok_count, wide), lambda i, first: (0, i, 0, 0)),
                w_spec,
                w_spec,
                pl.BlockSpec((rows, 2 * units), lambda i, first: (0, 0)),
                pl.BlockSpec((rows, units), lambda i, first: (0, 0)),
            ],
            out_specs=[pl.BlockSpec((rows, 2 * units), lambda i, first: (0, 0))] * 2,
            scratch_shapes=[pltpu.VMEM((local_experts, rows, head), jnp.bfloat16)],
        ),
        compiler_params=pltpu.CompilerParams(dimension_semantics=("arbitrary",)),
        cost_estimate=pl.CostEstimate(
            flops=2 * local_experts * rows * 2 * units * head + rows * BLOCK * head,
            bytes_accessed=20 << 20,
            transcendentals=0,
        ),
        name="head_products",
    )(first, x_all, w_gate, w_up, tail, hidden)


def hidden_kernel(*refs):
    *slot_refs, down_ref, out_ref = refs

    @pl.when(pl.program_id(0) == 0)
    def _():
        out_ref[...] = jnp.zeros_like(out_ref)

    rows = jnp.concatenate([ref[...] for ref in slot_refs], axis=0)
    out_ref[...] += lax.dot_general(rows, down_ref[0], NT, preferred_element_type=jnp.float32)


def slot_specs(parts, step, skip):
    return [pl.BlockSpec((part.shape[0], step), lambda k: (0, skip + k)) for part in parts]


def hidden_grads(e, parts, w_down):
    _, units, width = w_down.shape
    rows = sum(part.shape[0] for part in parts)
    return pl.pallas_call(
        hidden_kernel,
        out_shape=jax.ShapeDtypeStruct((rows, units), jnp.float32),
        grid=(width // STEP,),
        in_specs=slot_specs(parts, STEP, 0) + [pl.BlockSpec((1, units, STEP), lambda k: (e, 0, k))],
        out_specs=pl.BlockSpec((rows, units), lambda k: (0, 0)),
        compiler_params=pltpu.CompilerParams(dimension_semantics=("arbitrary",)),
        cost_estimate=pl.CostEstimate(flops=2 * rows * units * width, bytes_accessed=5 << 20, transcendentals=0),
        name="hidden_grads",
    )(*parts, w_down)


def tail_kernel(*refs):
    *slot_refs, gate_ref, up_ref, pre = refs
    units = gate_ref.shape[2]

    @pl.when(pl.program_id(0) == 0)
    def _():
        pre[...] = jnp.zeros_like(pre)

    rows = jnp.concatenate([ref[...] for ref in slot_refs], axis=0)
    pre[:, :units] += jnp.dot(rows, gate_ref[0], preferred_element_type=jnp.float32)
    pre[:, units:] += jnp.dot(rows, up_ref[0], preferred_element_type=jnp.float32)


def late_kernel(*refs):
    *slot_refs, hidden_ref, head_ref, gate_ref, up_ref, out_ref, pre = refs
    step = pl.program_id(0)
    units = gate_ref.shape[2]

    @pl.when(step == 0)
    def _():
        pre[...] = head_ref[...]

    rows = jnp.concatenate([ref[...] for ref in slot_refs], axis=0)
    pre[:, :units] += jnp.dot(rows, gate_ref[0], preferred_element_type=jnp.float32)
    pre[:, units:] += jnp.dot(rows, up_ref[0], preferred_element_type=jnp.float32)

    @pl.when(step == pl.num_programs(0) - 1)
    def _():
        unit_grads(pre[...], hidden_ref[...], out_ref)


def late_specs(e, parts, w_gate):
    _, width, units = w_gate.shape
    w_spec = pl.BlockSpec((1, TAIL_STEP, units), lambda k: (e, HEAD // TAIL_STEP + k, 0))
    rows = sum(part.shape[0] for part in parts)
    whole = pl.BlockSpec((rows, 2 * units), lambda k: (0, 0))
    cost = pl.CostEstimate(
        flops=4 * rows * units * (width - HEAD), bytes_accessed=6 << 20, transcendentals=rows * units
    )
    return slot_specs(parts, TAIL_STEP, width // TAIL_STEP), [w_spec, w_spec], whole, cost


def tail_products(e, parts, w_gate, w_up):
    slots, weights, whole, cost = late_specs(e, parts, w_gate)
    return pl.pallas_call(
        tail_kernel,
        out_shape=jax.ShapeDtypeStruct(whole.block_shape, jnp.float32),
        grid=((w_gate.shape[1] - HEAD) // TAIL_STEP,),
        in_specs=slots + weights,
        out_specs=whole,
        compiler_params=pltpu.CompilerParams(dimension_semantics=("arbitrary",)),
        cost_estimate=cost,
        name="tail_products",
    )(*parts, w_gate, w_up)


def late_grads(e, parts, hidden, head_pre, w_gate, w_up):
    slots, weights, whole, cost = late_specs(e, parts, w_gate)
    return pl.pallas_call(
        late_kernel,
        out_shape=jax.ShapeDtypeStruct(whole.block_shape, jnp.bfloat16),
        grid=((w_gate.shape[1] - HEAD) // TAIL_STEP,),
        in_specs=slots + [pl.BlockSpec(hidden.shape, lambda k: (0, 0)), whole] + weights,
        out_specs=whole,
        scratch_shapes=[pltpu.VMEM(whole.block_shape, jnp.float32)],
        compiler_params=pltpu.CompilerParams(dimension_semantics=("arbitrary",)),
        cost_estimate=cost,
        name="late_grads",
    )(*parts, hidden, head_pre, w_gate, w_up)


def out_kernel(h0_ref, h1_ref, gate_ref, up_ref, *out_refs):
    units = gate_ref.shape[2]
    for e, h_ref in enumerate((h0_ref, h1_ref)):
        value = lax.dot_general(h_ref[:, :units], gate_ref[e], NT, preferred_element_type=jnp.float32)
        value = value + lax.dot_general(h_ref[:, units:], up_ref[e], NT, preferred_element_type=jnp.float32)
        value = value.astype(jnp.bfloat16)
        part = value.shape[0] // 4
        first = 0
        for out_ref in out_refs:
            last = first + out_ref.shape[0]
            group = first // (2 * part)
            start, stop = first - group * 2 * part, last - group * 2 * part
            low, high = max(start, e * part), min(stop, (e + 1) * part)
            if low < high:
                at = group * part - e * part
                out_ref[low - start : high - start, :] = value[at + low : at + high]
            first = last


def out_rows(h, w_gate, w_up, start, stop, step, counts):
    rows = h[0].shape[0]
    local_experts, width, units = w_gate.shape
    h_spec = pl.BlockSpec((rows, 2 * units), lambda n: (0, 0))
    w_spec = pl.BlockSpec((local_experts, step, units), lambda n: (0, start // step + n, 0))
    return pl.pallas_call(
        out_kernel,
        out_shape=[jax.ShapeDtypeStruct((count, stop - start), jnp.bfloat16) for count in counts],
        grid=((stop - start) // step,),
        in_specs=[h_spec, h_spec, w_spec, w_spec],
        out_specs=[pl.BlockSpec((count, step), lambda n: (0, n)) for count in counts],
        compiler_params=pltpu.CompilerParams(dimension_semantics=("arbitrary",)),
        cost_estimate=pl.CostEstimate(
            flops=2 * local_experts * rows * 2 * units * (stop - start), bytes_accessed=8 << 20, transcendentals=0
        ),
        name="out_rows",
    )(*h, w_gate, w_up)


def total(*terms):
    value = terms[0].astype(jnp.float32)
    for term in terms[1:]:
        value = value + term.astype(jnp.float32)
    return value.astype(jnp.bfloat16)


def on_device(tokens, out_grad, route_ids, route_probs, w_gate, w_up, w_down):
    columns = lax.axis_size("expert")
    local_experts = w_gate.shape[0]
    experts = local_experts * columns
    tok_count, width = tokens.shape
    slots = experts * CAP
    per_dest = local_experts * CAP
    first = (lax.axis_index("expert").astype(jnp.int32) * local_experts).reshape(1)

    up_ring = [(i, (i + 1) % 4) for i in range(4)]
    down_ring = [(i, (i + 3) % 4) for i in range(4)]
    far_ring = [(i, (i + 2) % 4) for i in range(4)]

    with jax.named_scope("gather_tokens"):
        ids = jnp.pad(route_ids.astype(jnp.bfloat16), ((0, 0), (0, LANES - route_ids.shape[1])), constant_values=-1)
        mine = jnp.concatenate([tokens[:, :HEAD], ids], axis=1)
        pieces = [mine] + [lax.ppermute(mine, "dp", ring) for ring in (down_ring, far_ring, up_ring)]

    with jax.named_scope("build_slots"):
        table, slot_scale = slot_table(route_ids, route_probs, experts)
        select = table.astype(jnp.bfloat16)
        tiles = []
        for e in range(2):
            choose = select.reshape(columns, local_experts, CAP, tok_count)[:, e].reshape(columns * CAP, tok_count)
            scale = slot_scale.reshape(columns, local_experts, CAP)[:, e].reshape(columns * CAP, 1)
            g_rows = jnp.dot(choose, out_grad, preferred_element_type=jnp.float32) * scale
            x_rows = jnp.dot(choose, tokens[:, HEAD:], preferred_element_type=jnp.float32)
            rows = jnp.concatenate([g_rows.astype(jnp.bfloat16), x_rows.astype(jnp.bfloat16)], axis=1)
            tiles.append(rows.reshape(columns, CAP, -1))

    with jax.named_scope("gather_tokens"):
        tiles[0], pieces = lax.optimization_barrier((tiles[0], pieces))
        near = jnp.concatenate(pieces)
        x_all = lax.all_gather(near, "expert", axis=0, tiled=True).reshape(columns, 4, tok_count, HEAD + LANES)

    def unpack(got):
        got = got.transpose(1, 0, 2)
        return [got[0], got[1]]

    def send(slab):
        return lax.all_to_all(slab, "expert", split_axis=0, concat_axis=0, tiled=True)

    def ring(own):
        right1 = lax.ppermute(own[1], "dp", down_ring)
        left0 = lax.ppermute(own[0], "dp", up_ring)
        right0 = lax.ppermute(own[0], "dp", down_ring)
        left1 = lax.ppermute(own[1], "dp", up_ring)
        return [right0, right1], [left0, left1]

    def ring_on(left0, right1):
        return [lax.ppermute(left0, "dp", up_ring), lax.ppermute(right1, "dp", down_ring)]

    with jax.named_scope("first_expert"):
        own = unpack(send(tiles[0]))
        right, left = ring(own)
        far = ring_on(left[0], right[1])
    with jax.named_scope("second_expert"):
        slab, _ = lax.optimization_barrier((tiles[1], own[0]))
        got, right, left, far = lax.optimization_barrier((send(slab), right, left, far))
        first_parts = own + right + far + left
        hidden0 = hidden_grads(0, first_parts, w_down)
        tail0 = tail_products(0, first_parts, w_gate, w_up)
        own = unpack(got)
        right, left = ring(own)
        left[0], right[1], hidden0, tail0 = lax.optimization_barrier((left[0], right[1], hidden0, tail0))
        far = ring_on(left[0], right[1])
        h0, head_pre = head_products(first, x_all, w_gate, w_up, tail0, hidden0)
        far, left[1], right[0], h0 = lax.optimization_barrier((far, left[1], right[0], h0))
        second_parts = own + right + far + left

    hidden1 = hidden_grads(1, second_parts, w_down)
    h = [h0, late_grads(1, second_parts, hidden1, head_pre, w_gate, w_up)]

    few, many = slots // 4, slots - slots // 4
    own_a, right_a, far_a, left_a = out_rows(h, w_gate, w_up, 0, OUT_SPLIT, 640, [slots] * 4)
    own_b0, own_b1, right_b0, right_b1, far_b0, far_b1, left_b0, left_b1 = out_rows(
        h, w_gate, w_up, OUT_SPLIT, width, 256, [few, many] * 4
    )
    with jax.named_scope("sum_blocks"):
        from_far = lax.ppermute(far_a, "dp", up_ring)
        from_right_a = lax.ppermute(left_a, "dp", down_ring)
        from_left_a = lax.ppermute(total(right_a, from_far), "dp", up_ring)
        far_b1, left_b0, from_right_a = lax.optimization_barrier((far_b1, left_b0, from_right_a))
        from_far1 = lax.ppermute(far_b1, "dp", down_ring)
        from_right_b0 = lax.ppermute(left_b0, "dp", down_ring)
        far_b0, right_b1, from_left_a = lax.optimization_barrier((far_b0, right_b1, from_left_a))
        from_far0 = lax.ppermute(far_b0, "dp", up_ring)
        from_left_b1 = lax.ppermute(right_b1, "dp", up_ring)
        left_b1, from_left_a = lax.optimization_barrier((total(left_b1, from_far1), from_left_a))
        from_right_b1 = lax.ppermute(left_b1, "dp", down_ring)
        from_left_b0 = lax.ppermute(total(right_b0, from_far0), "dp", up_ring)

    sums_a = total(own_a, from_left_a, from_right_a)
    sums_b = jnp.concatenate(
        [total(own_b0, from_left_b0, from_right_b0), total(own_b1, from_left_b1, from_right_b1)], axis=0
    )
    results = []
    for summed in (sums_a, sums_b):
        with jax.named_scope("return_slots"):
            cols = summed.shape[1]
            back = summed.reshape(per_dest, columns, cols).transpose(1, 0, 2)
            returned = lax.all_to_all(back, "expert", split_axis=0, concat_axis=0, tiled=True)
        with jax.named_scope("combine"):
            results.append(
                lax.dot_general(
                    select, returned.reshape(slots, cols), (((0,), (0,)), ((), ())),
                    preferred_element_type=jnp.float32,
                ).astype(jnp.bfloat16)
            )
    return jnp.concatenate(results, axis=1)


def solution(mesh):
    placed = (
        P(("dp", "expert"), None),
        P(("dp", "expert"), None),
        P(("dp", "expert"), None),
        P(("dp", "expert"), None),
        P("expert", None, "dp"),
        P("expert", None, "dp"),
        P("expert", "dp", None),
    )
    return jax.shard_map(
        on_device, mesh=mesh, in_specs=placed, out_specs=P(("dp", "expert"), None), check_vma=False
    )
```
